32 devices in a mesh: groups: 2 (over y), sensor: 4 (over z), tm: 4 (over x, core).
Axes of the slice: x: 2, y: 2, z: 4, core: 2. Of those that a mesh axis runs over, the one named last changes fastest.
Arguments:
- series: bfloat16 [16, 64, 16384], P('tm', None, ('groups', 'sensor')), parts along dimension 2, may hold values from -6 to 6
- neighbours: int32 [64, 4], P(('groups', 'sensor')), parts along dimension 0, may hold values from 0 to 31, as said below
- tile_count: int32 [64], P(('groups', 'sensor')), parts along dimension 0, may hold values from 1 to 4
- tiles: bfloat16 [64, 4, 256, 256], P(('groups', 'sensor')), parts along dimension 0, may hold values from -0.25 to 0.25
- filter_gate_weight: bfloat16 [2, 2, 128, 64], replicated, may hold values from -0.5 to 0.5
- filter_gate_bias: float32 [2, 128], replicated, may hold values from -3 to 3
- skip_weight: bfloat16 [2, 256, 64], replicated, may hold values from -0.75 to 0.75
- skip_b: float32 [2, 256], replicated, may hold values from -3 to 3
- hop_mixing_weight: bfloat16 [2, 64, 192], replicated, may hold values from -0.4375 to 0.4375
- mix_b: float32 [2, 64], replicated, may hold values from -3 to 3
Outputs:
- stream: bfloat16 [16, 64, 16384], P('tm', None, ('groups', 'sensor')), parts along dimension 2
- skip_sum: bfloat16 [16, 256, 16384], P('tm', None, ('groups', 'sensor')), parts along dimension 2
The draws below stay inside these ranges and needn't reach their ends.
There are 2 independent parts, one for each index of `groups`. The reference program is written for one: setup_inputs(seed, part) draws one part's arguments, and reference() takes and returns one part's arrays. A program takes and returns all parts, laid end to end along the dimension named above; an argument that names none is the same for every part. Nothing has to cross between parts.
Inputs may be any that keep to these rules, and one draw needn't show every extreme that they name: `neighbours`: global block ids of the part. Entry k of row b is used only for k < tile_count[b]. Used entries name blocks of the row's own shard or of shards 1 or 2 away along sensor, wrapping around. Over the rows of one shard of 8 blocks, the used entries that lie on any one other shard name at most 2 distinct blocks, and every shard reaches 2 for some other shard.
All inputs are finite; a program needn't handle non-finite values.
Results may differ from the reference program's by a relative error of at most 0.0055.
Values may be sent and summed in bfloat16 or wider, within the bound.
A program may use at most 128 MiB of HBM per device.

```python
import jax
import jax.numpy as jnp

RESIDUAL_WIDTH = 64
DILATION_WIDTH = 64
SKIP_WIDTH = 256
TILE = 256
MAXT = 4
GATED_LAYERS = 2
BLK_DEV = 8
NBLK = 32
NODES = 8192
TIME = 16
N_SENSOR = 4


def graph_layout(key):
    blocks = BLK_DEV
    shards = N_SENSOR
    total_blocks = blocks * shards
    rows = jnp.arange(total_blocks, dtype=jnp.int32)
    owner = rows // blocks
    within = rows % blocks
    offsets = jax.random.randint(jax.random.fold_in(key, 11), (shards, shards), 0, blocks).astype(jnp.int32)
    side_one = jax.random.randint(jax.random.fold_in(key, 12), (total_blocks,), 0, 2).astype(jnp.int32)
    side_two = jax.random.randint(jax.random.fold_in(key, 13), (total_blocks,), 0, 2).astype(jnp.int32)
    pick_one = jax.random.randint(jax.random.fold_in(key, 17), (total_blocks,), 0, 2).astype(jnp.int32)
    pick_two = jax.random.randint(jax.random.fold_in(key, 18), (total_blocks,), 0, 2).astype(jnp.int32)
    forced = jax.random.randint(jax.random.fold_in(key, 14), (shards,), 0, blocks).astype(jnp.int32)
    is_first = within == forced[owner]
    is_second = within == (forced[owner] + 1) % blocks
    is_forced = is_first | is_second
    step_one = jnp.where(is_forced, 1, 2 * side_one - 1).astype(jnp.int32)
    pick_one = jnp.where(is_first, 0, jnp.where(is_second, 1, pick_one)).astype(jnp.int32)
    step_two = (4 * side_two - 2).astype(jnp.int32)
    peer_one = (owner + step_one + shards) % shards
    peer_two = (owner + step_two + 2 * shards) % shards
    near = owner * blocks + jax.random.randint(jax.random.fold_in(key, 15), (total_blocks,), 0, blocks).astype(jnp.int32)
    far_one = peer_one * blocks + (offsets[owner, peer_one] + pick_one) % blocks
    far_two = peer_two * blocks + (offsets[owner, peer_two] + pick_two) % blocks
    counts = jax.random.randint(jax.random.fold_in(key, 16), (total_blocks,), 3, MAXT + 1).astype(jnp.int32)
    counts = jnp.where(is_forced, MAXT, counts)
    single = (owner == 0) & (within == (forced[0] + 2) % blocks)
    counts = jnp.where(single, 1, counts).astype(jnp.int32)
    table = jnp.stack([rows, near, far_one, far_two], 1).astype(jnp.int32)
    used = jnp.arange(MAXT, dtype=jnp.int32)[None, :] < counts[:, None]
    table = jnp.where(used, table, rows[:, None]).astype(jnp.int32)
    return (table, counts)


def draw_neighbours(key, part):
    table, counts = graph_layout(key)
    return table


def draw_tile_count(key, part):
    table, counts = graph_layout(key)
    return counts


def block_levels(stream_key, shape, split, smallest, largest):
    gain = 1.0
    for axis_at, shards_of in split:
        heights = jax.random.uniform(jax.random.fold_in(jax.random.fold_in(stream_key, 6), axis_at), (shards_of,), jnp.float32, smallest / len(split), largest / len(split))
        gain = gain * jnp.repeat(jnp.exp(heights), shape[axis_at] // shards_of).reshape((-1,) + (1,) * (len(shape) - 1 - axis_at))
    return gain


def gaussian(rng, shape, spread, most, split=(), held_as=jnp.bfloat16):
    array = jax.random.normal(rng, shape, jnp.float32) * spread
    if len(split) > 0:
        array = block_levels(rng, shape, split, -0.22, 0.18) * array
    return jnp.clip(array, min=-most, max=most).astype(held_as)


def setup_inputs(seed: int = 0, part: int = 0) -> dict:
    key_list = jax.random.split(jax.random.key(seed), 11)
    part_splits = jax.random.split(jax.random.fold_in(key_list[10], part), 11)
    series = gaussian(part_splits[0], (TIME, RESIDUAL_WIDTH, NODES), 1.0, 6.0, ((0, 4), (2, 4)))
    neighbours = draw_neighbours(jax.random.fold_in(jax.random.fold_in(key_list[10], part), 71), part)
    tile_count = draw_tile_count(jax.random.fold_in(jax.random.fold_in(key_list[10], part), 71), part)
    tiles = gaussian(part_splits[3], (NBLK, MAXT, TILE, TILE), (2 * TILE) ** -0.5, 0.25, ((0, 4),))
    filter_gate_weight = gaussian(key_list[4], (GATED_LAYERS, 2, 2 * DILATION_WIDTH, RESIDUAL_WIDTH), (2 * RESIDUAL_WIDTH) ** -0.5, 0.5)
    filter_gate_bias = gaussian(key_list[5], (GATED_LAYERS, 2 * DILATION_WIDTH), 0.5, 3.0, (), jnp.float32)
    skip_weight = gaussian(key_list[6], (GATED_LAYERS, SKIP_WIDTH, DILATION_WIDTH), DILATION_WIDTH ** -0.5, 0.75)
    skip_b = gaussian(key_list[7], (GATED_LAYERS, SKIP_WIDTH), 0.5, 3.0, (), jnp.float32)
    hop_mixing_weight = gaussian(key_list[8], (GATED_LAYERS, RESIDUAL_WIDTH, 3 * DILATION_WIDTH), (3 * DILATION_WIDTH) ** -0.5, 0.4375)
    mix_b = gaussian(key_list[9], (GATED_LAYERS, RESIDUAL_WIDTH), 0.5, 3.0, (), jnp.float32)
    return dict(series=series, neighbours=neighbours, tile_count=tile_count, tiles=tiles, filter_gate_weight=filter_gate_weight, filter_gate_bias=filter_gate_bias, skip_weight=skip_weight, skip_b=skip_b, hop_mixing_weight=hop_mixing_weight, mix_b=mix_b)


def gated(prev, cur, filter_gate_weight, filter_gate_bias, layer):
    preceding_input = jnp.einsum("or,trn->ton", filter_gate_weight[layer, 0].astype(jnp.float32), prev.astype(jnp.float32))
    preceding_input = preceding_input + jnp.einsum("or,trn->ton", filter_gate_weight[layer, 1].astype(jnp.float32), cur.astype(jnp.float32))
    preceding_input = preceding_input + filter_gate_bias[layer][None, :, None]
    return (jnp.tanh(preceding_input[:, :DILATION_WIDTH]) * jax.nn.sigmoid(preceding_input[:, DILATION_WIDTH:])).astype(jnp.bfloat16)


def diffuse(field, neighbours, tile_count, tiles):
    count_blocks = neighbours.shape[0]
    view = field.reshape(-1, count_blocks, TILE).astype(jnp.float32)
    live = (jnp.arange(MAXT)[None, :] < tile_count[:, None]).astype(jnp.float32)
    total = jnp.zeros(view.shape, jnp.float32)
    for slot in range(MAXT):
        source = view[:, neighbours[:, slot], :]
        term = jnp.einsum("rbj,bji->rbi", source, tiles[:, slot].astype(jnp.float32))
        total = total + live[:, slot][None, :, None] * term
    return total.reshape(field.shape).astype(jnp.bfloat16)


def reference(series, neighbours, tile_count, tiles, filter_gate_weight, filter_gate_bias, skip_weight, skip_b, hop_mixing_weight, mix_b):
    state = series
    skip_total = jnp.zeros((series.shape[0], SKIP_WIDTH, series.shape[2]), jnp.float32)
    for layer in range(GATED_LAYERS):
        reach = 2 ** layer
        prev = jnp.concatenate([jnp.zeros((reach,) + state.shape[1:], state.dtype), state[:-reach]], 0)
        hidden = gated(prev, state, filter_gate_weight, filter_gate_bias, layer)
        skip_total = skip_total + jnp.einsum("sd,tdn->tsn", skip_weight[layer].astype(jnp.float32), hidden.astype(jnp.float32)) + skip_b[layer][None, :, None]
        first_hop = diffuse(hidden, neighbours, tile_count, tiles)
        second_hop = diffuse(first_hop, neighbours, tile_count, tiles)
        stacked = jnp.concatenate([hidden, first_hop, second_hop], 1).astype(jnp.float32)
        mixed = jnp.einsum("rc,tcn->trn", hop_mixing_weight[layer].astype(jnp.float32), stacked) + mix_b[layer][None, :, None]
        state = (state.astype(jnp.float32) + mixed).astype(jnp.bfloat16)
    return state, skip_total.astype(jnp.bfloat16)
```

```python
import functools

import jax
import jax.numpy as jnp
from jax import lax
from jax.experimental import pallas as pl
from jax.experimental.pallas import tpu as pltpu
from jax.sharding import PartitionSpec as P

CAP = 2
LAYERS = 2
HOPS = 2
UNROLL = 8
MESH = pl.DeviceIdType.MESH
F32 = jnp.float32
BF16 = jnp.bfloat16


def offsets_of(shards):
    found = []
    for step in (2, shards - 2, 1, shards - 1):
        step = step % shards
        if step and step not in found:
            found.append(step)
    return found


def order_of(steps):
    return list(range(steps - 2, -1, -2)) + list(range(steps - 1, -1, -2))


def body(
    shards,
    ranks,
    near_hbm,
    count_hbm,
    series_hbm,
    tiles_hbm,
    fgw_hbm,
    fgb_hbm,
    sw_hbm,
    sb_hbm,
    hmw_hbm,
    mb_hbm,
    outv,
    skipv,
    tiles_v,
    place_v,
    base_last,
    pool_last,
    near,
    count,
    tab_v,
    tab_r,
    src,
    series,
    fgw,
    fgb_row,
    sw,
    sb_row,
    hmw,
    mb_row,
    fgb,
    sb,
    mb,
    x1,
    edge0,
    edge1,
    fields,
    mid,
    base,
    hs,
    sendb,
    wg,
    wm,
    ws,
    tiles_sem,
    load_sem,
    series_sem,
    tab_send,
    tab_recv,
    place_sem,
    edge_send,
    edge_recv,
    usend,
    urecv,
    *pools,
):
    steps, chan, nodes = series.shape
    blocks, maxt, width = tiles_v.shape[0], tiles_v.shape[1], tiles_v.shape[2]
    offs = offsets_of(shards)
    order = order_of(steps)
    me = lax.axis_index("sensor")
    tm = lax.axis_index("tm")
    peers = [lax.rem(me + off, shards) for off in offs]
    mirror = [offs.index(shards - off) for off in offs]
    after = lax.rem(tm + 1, ranks)
    dead = blocks + CAP * len(offs)
    last = LAYERS * HOPS * steps - 1

    def unit(layer, hop, t):
        return (layer * HOPS + hop) * steps + order.index(t)

    def pool_of(u):
        return pool_last if u == last else pools[u]

    barrier = pltpu.get_barrier_semaphore()
    for peer in peers:
        pl.semaphore_signal(barrier, inc=1, device_id={"sensor": peer}, device_id_type=MESH)
    around = sorted({1 % ranks, (ranks - 1) % ranks} - {0})
    for step in around:
        pl.semaphore_signal(
            barrier, inc=1, device_id={"tm": lax.rem(tm + step, ranks)}, device_id_type=MESH
        )

    loads = [
        pltpu.make_async_copy(held, into, load_sem.at[i])
        for i, (held, into) in enumerate(
            (
                (near_hbm, near),
                (count_hbm, count),
                (fgw_hbm, fgw),
                (fgb_hbm, fgb_row),
                (hmw_hbm, hmw),
                (mb_hbm, mb_row),
                (sw_hbm, sw),
                (sb_hbm, sb_row),
            )
        )
    ]
    parts = [
        pltpu.make_async_copy(series_hbm.at[t], series.at[t], series_sem.at[t])
        for t in range(steps)
    ]
    soon = [order[0], order[0] - 1]
    for copy in loads[:2]:
        copy.start()
    for t in soon:
        parts[t].start()
    for copy in loads[2:6]:
        copy.start()
    for t in range(steps - 1, -1, -1):
        if t not in soon:
            parts[t].start()
    for copy in loads[6:]:
        copy.start()
    tiles_in = pltpu.make_async_copy(tiles_hbm, tiles_v, tiles_sem)

    loads[0].wait()
    loads[1].wait()
    slot = lax.broadcasted_iota(jnp.int32, near.shape, 0)
    tab_v[...] = jnp.full(tab_v.shape, -1, jnp.int32)
    tab_v[0:maxt, 0:blocks] = jnp.where(slot < count[...], near[...], -1)

    pl.semaphore_wait(barrier, len(peers) + len(around))

    tables = []
    for o, peer in enumerate(peers):
        copy = pltpu.make_async_remote_copy(
            src_ref=tab_v,
            dst_ref=tab_r.at[mirror[o]],
            send_sem=tab_send.at[o],
            recv_sem=tab_recv.at[mirror[o]],
            device_id={"sensor": peer},
            device_id_type=MESH,
        )
        copy.start()
        tables.append(copy)

    for copy in loads[2:6]:
        copy.wait()

    def upright(row):
        tall = jnp.transpose(jnp.broadcast_to(row, (128, 128)))
        return jnp.concatenate([tall] * (width // 128), axis=1)

    def flipped(parts):
        return jnp.transpose(jnp.concatenate(parts, axis=0).astype(F32)).astype(BF16)

    both_mix = upright(jnp.concatenate([mb_row[pl.ds(i, 1), :] for i in range(LAYERS)], axis=1))
    for layer in range(LAYERS):
        mb[layer] = both_mix[layer * chan : (layer + 1) * chan]

    def prepare(layer):
        fgb[layer] = upright(fgb_row[pl.ds(layer, 1), :])
        wg[layer] = flipped([fgw[layer, 0], fgw[layer, 1]])
        w = hmw[layer]
        for i in range(3):
            wm[layer, i * chan : (i + 1) * chan] = w[:, (2 - i) * chan : (3 - i) * chan]

    prepare(0)
    for t in soon:
        parts[t].wait()

    def columns(b):
        return pl.ds(pl.multiple_of(b * width, width), width)

    def gate(layer, t):
        reach = 2**layer
        field = series if layer == 0 else x1
        u = unit(layer, 0, t)
        final = unit(layer, 1, t) == last

        def per_block(b, carry):
            cols = columns(b)
            cur = field[t, :, cols]
            if t >= reach:
                prev = field[t - reach, :, cols]
            else:
                held = edge0[:, cols] if layer == 0 else edge1[t, :, cols]
                prev = lax.select(tm > 0, held, jnp.zeros_like(held))
            both = jnp.concatenate([prev, cur], axis=0)
            pre = jnp.dot(wg[layer], both, preferred_element_type=F32) + fgb[layer]
            half = pre.shape[0] // 2
            h = jnp.tanh(pre[:half]) * (0.5 * jnp.tanh(0.5 * pre[half:]) + 0.5)
            h = h.astype(BF16)
            hs[t, b, layer * chan : (layer + 1) * chan] = h
            three = jnp.dot(wm[layer], h, preferred_element_type=F32)
            v = three[0:chan].astype(BF16)
            fields[t, b] = v
            pool_of(u)[b] = v
            mid[t, b] = three[chan : 2 * chan]
            rest = cur.astype(F32) + (three[2 * chan : 3 * chan] + mb[layer])
            if final:
                base_last[b] = rest
            else:
                base[t, b] = rest
            return carry

        lax.fori_loop(0, blocks, per_block, 0, unroll=UNROLL)

    def moves(layer, hop, t):
        u = unit(layer, hop, t)
        return [
            pltpu.make_async_remote_copy(
                src_ref=sendb.at[u, o],
                dst_ref=pool_of(u).at[pl.ds(blocks + CAP * mirror[o], CAP)],
                send_sem=usend.at[u, o],
                recv_sem=urecv.at[u, mirror[o]],
                device_id={"sensor": peer},
                device_id_type=MESH,
            )
            for o, peer in enumerate(peers)
        ]

    def arrive(layer, hop, t):
        u = unit(layer, hop, t)
        for o, peer in enumerate(peers):
            pltpu.make_async_remote_copy(
                src_ref=sendb.at[u, o],
                dst_ref=pool_of(u).at[pl.ds(blocks + CAP * o, CAP)],
                send_sem=usend.at[u, o],
                recv_sem=urecv.at[u, o],
                device_id={"sensor": peer},
                device_id_type=MESH,
            ).wait_recv()

    def send(layer, hop, t):
        u = unit(layer, hop, t)
        copies = moves(layer, hop, t)
        for o in range(len(peers)):
            for s in range(CAP):
                sendb[u, o, s] = fields[t, want[o][s]]
            copies[o].start()

    def diffuse(layer, hop, t):
        u = unit(layer, hop, t)

        def per_block(b, carry):
            picked = [pool_of(u)[src[k, b]] for k in range(maxt)]
            stack = jnp.concatenate(picked, axis=1)
            held = tiles_v[b].reshape(maxt * width, width)
            total = jnp.dot(stack, held, preferred_element_type=F32)
            if hop == 0:
                a = (mid[t, b] + total).astype(BF16)
                fields[t, b] = a
                pool_of(unit(layer, 1, t))[b] = a
            else:
                nxt = (base[t, b] + total).astype(BF16)
                into = x1 if layer == 0 else outv
                into[t, :, columns(b)] = nxt
            return carry

        lax.fori_loop(0, blocks, per_block, 0, unroll=UNROLL)

    def skip(t):
        def per_block(b, carry):
            out = jnp.dot(ws[...], hs[t, b], preferred_element_type=F32) + sb[...]
            skipv[t, :, columns(b)] = out.astype(BF16)
            return carry

        lax.fori_loop(0, blocks, per_block, 0, unroll=UNROLL)

    def bounds(table, low):
        rel = table - low
        mine = (rel >= 0) & (rel < blocks)
        return rel, mine

    gate(0, order[0])

    want = []
    for o, peer in enumerate(peers):
        pltpu.make_async_remote_copy(
            src_ref=tab_v,
            dst_ref=tab_r.at[o],
            send_sem=tab_send.at[o],
            recv_sem=tab_recv.at[o],
            device_id={"sensor": peer},
            device_id_type=MESH,
        ).wait_recv()
        rel, mine = bounds(tab_r[o], me * blocks)
        least = jnp.min(jnp.where(mine, rel, blocks))
        most = jnp.max(jnp.where(mine, rel, -1))
        want.append((jnp.where(least < blocks, least, 0), jnp.maximum(most, 0)))

    send(0, 0, order[0])
    parts[steps - 1].wait()
    first_edge = pltpu.make_async_remote_copy(
        src_ref=series.at[steps - 1],
        dst_ref=edge0,
        send_sem=edge_send.at[0],
        recv_sem=edge_recv.at[0],
        device_id={"tm": after},
        device_id_type=MESH,
    )
    first_edge.start()
    tiles_in.start()
    for t in range(steps):
        if t != steps - 1 and t not in soon:
            parts[t].wait()
    for copy in loads[6:]:
        copy.wait()
    later_edges = [
        pltpu.make_async_remote_copy(
            src_ref=x1.at[steps - 2 + i],
            dst_ref=edge1.at[i],
            send_sem=edge_send.at[1 + i],
            recv_sem=edge_recv.at[1 + i],
            device_id={"tm": after},
            device_id_type=MESH,
        )
        for i in range(2)
    ]

    table = tab_v[...]
    rel, mine = bounds(table, me * blocks)
    place = jnp.where(mine, rel, dead)
    for o, peer in enumerate(peers):
        rel, mine = bounds(table, peer * blocks)
        least = jnp.min(jnp.where(mine, rel, blocks), axis=(0, 1), keepdims=True)
        place = jnp.where(mine, blocks + CAP * o + jnp.where(rel == least, 0, 1), place)
    place_v[...] = place
    places = pltpu.make_async_copy(place_v, src, place_sem)
    places.start()

    waited = False
    for t in order[1:]:
        if t == 0 and not waited:
            first_edge.wait_recv()
            waited = True
        gate(0, t)
        send(0, 0, t)

    for u in range(last + 1):
        pool_of(u)[dead] = jnp.zeros((chan, width), BF16)
    for layer in range(1, LAYERS):
        prepare(layer)
    ws[...] = flipped([sw[layer] for layer in range(LAYERS)])
    row = sb_row[0:1, :]
    for layer in range(1, LAYERS):
        row = row + sb_row[pl.ds(layer, 1), :]
    for at in range(0, row.shape[1], 128):
        sb[at : at + 128] = upright(row[:, at : at + 128])

    places.wait()
    tiles_in.wait()
    for t in order:
        arrive(0, 0, t)
        diffuse(0, 0, t)
        send(0, 1, t)
    for t in order:
        arrive(0, 1, t)
        diffuse(0, 1, t)
        if t >= steps - 2:
            later_edges[t - (steps - 2)].start()
        else:
            gate(1, t + 2)
            send(1, 0, t + 2)
        if t < 2:
            later_edges[t].wait_recv()
            gate(1, t)
            send(1, 0, t)
    for t in order:
        skip(t)
    for t in order:
        arrive(1, 0, t)
        diffuse(1, 0, t)
        send(1, 1, t)
    for t in order[:-1]:
        arrive(1, 1, t)
        diffuse(1, 1, t)

    for copy in tables:
        copy.wait_send()
    first_edge.wait_send()
    for copy in later_edges:
        copy.wait_send()
    for layer in range(LAYERS):
        for hop in range(HOPS):
            for t in order:
                if unit(layer, hop, t) != last:
                    for copy in moves(layer, hop, t):
                        copy.wait_send()
    arrive(1, 1, order[-1])
    for copy in moves(1, 1, order[-1]):
        copy.wait_send()


def finish(
    outv, skipv, tiles_v, place_v, base, pool, stream, skip_sum, src, tail, sems
):
    steps, chan, nodes = outv.shape
    blocks, maxt, width = tiles_v.shape[0], tiles_v.shape[1], tiles_v.shape[2]
    order = order_of(steps)
    places = pltpu.make_async_copy(place_v, src, sems.at[0])
    places.start()
    copies = [pltpu.make_async_copy(skipv, skip_sum, sems.at[1])]
    for i, t in enumerate(order[:-1]):
        copies.append(pltpu.make_async_copy(outv.at[t], stream.at[t], sems.at[2 + i]))
    for copy in copies:
        copy.start()
    places.wait()

    def per_block(b, carry):
        stack = jnp.concatenate([pool[src[k, b]] for k in range(maxt)], axis=1)
        held = tiles_v[b].reshape(maxt * width, width)
        total = jnp.dot(stack, held, preferred_element_type=F32)
        cols = pl.ds(pl.multiple_of(b * width, width), width)
        tail[:, cols] = (base[b] + total).astype(BF16)
        return carry

    lax.fori_loop(0, blocks, per_block, 0, unroll=UNROLL)
    final = pltpu.make_async_copy(tail, stream.at[order[-1]], sems.at[1 + steps])
    final.start()
    for copy in copies:
        copy.wait()
    final.wait()


def solution(mesh):
    shards, ranks = mesh.shape["sensor"], mesh.shape["tm"]
    links = len(offsets_of(shards))

    def on_device(
        series, neighbours, tile_count, tiles, fgw, fgb, skip_weight, skip_b, hop_mixing, mix_b
    ):
        steps, chan, nodes = series.shape
        blocks, maxt, width = tiles.shape[0], tiles.shape[1], tiles.shape[2]
        wide = skip_weight.shape[1]
        pool = blocks + CAP * links + 1
        units = LAYERS * HOPS * steps
        fgw_t = jnp.swapaxes(fgw, 2, 3)
        skip_t = jnp.swapaxes(skip_weight, 1, 2)
        operands = [
            pltpu.with_memory_space_constraint(held, pltpu.HBM)
            for held in (
                neighbours.T,
                tile_count[None, :],
                series,
                tiles,
                fgw_t,
                fgb,
                skip_t,
                skip_b,
                hop_mixing,
                mix_b,
            )
        ]
        vmem = pl.BlockSpec(memory_space=pltpu.VMEM)
        hbm = pl.BlockSpec(memory_space=pltpu.HBM)
        dma = pltpu.SemaphoreType.DMA
        results = (
            jax.ShapeDtypeStruct(series.shape, BF16),
            jax.ShapeDtypeStruct((steps, wide, nodes), BF16),
        )
        held = pl.pallas_call(
            functools.partial(body, shards, ranks),
            out_shape=results
            + (
                jax.ShapeDtypeStruct(tiles.shape, BF16),
                jax.ShapeDtypeStruct((8, 128), jnp.int32),
                jax.ShapeDtypeStruct((blocks, chan, width), F32),
                jax.ShapeDtypeStruct((pool, chan, width), BF16),
            ),
            in_specs=[hbm] * 10,
            out_specs=(vmem,) * 6,
            scratch_shapes=[
                pltpu.VMEM((maxt, blocks), jnp.int32),
                pltpu.VMEM((1, blocks), jnp.int32),
                pltpu.VMEM((8, 128), jnp.int32),
                pltpu.VMEM((links, 8, 128), jnp.int32),
                pltpu.SMEM((8, 128), jnp.int32),
                pltpu.VMEM(series.shape, BF16),
                pltpu.VMEM(fgw_t.shape, BF16),
                pltpu.VMEM(fgb.shape, F32),
                pltpu.VMEM(skip_t.shape, BF16),
                pltpu.VMEM(skip_b.shape, F32),
                pltpu.VMEM(hop_mixing.shape, BF16),
                pltpu.VMEM(mix_b.shape, F32),
                pltpu.VMEM((LAYERS, 2 * chan, width), F32),
                pltpu.VMEM((wide, width), F32),
                pltpu.VMEM((LAYERS, chan, width), F32),
                pltpu.VMEM(series.shape, BF16),
                pltpu.VMEM((chan, nodes), BF16),
                pltpu.VMEM((2, chan, nodes), BF16),
                pltpu.VMEM((steps, blocks, chan, width), BF16),
                pltpu.VMEM((steps, blocks, chan, width), F32),
                pltpu.VMEM((steps, blocks, chan, width), F32),
                pltpu.VMEM((steps, blocks, LAYERS * chan, width), BF16),
                pltpu.VMEM((units, links, CAP, chan, width), BF16),
                pltpu.VMEM((LAYERS, 2 * chan, 2 * chan), BF16),
                pltpu.VMEM((LAYERS, 3 * chan, chan), BF16),
                pltpu.VMEM((wide, LAYERS * chan), BF16),
                dma,
                dma((8,)),
                dma((steps,)),
                dma((links,)),
                dma((links,)),
                dma,
                dma((3,)),
                dma((3,)),
                dma((units, links)),
                dma((units, links)),
            ]
            + [pltpu.VMEM((pool, chan, width), BF16)] * (units - 1),
            compiler_params=pltpu.CompilerParams(
                collective_id=0, has_side_effects=True, vmem_limit_bytes=40 << 20
            ),
        )(*operands)
        return pl.pallas_call(
            finish,
            out_shape=results,
            in_specs=[vmem] * 6,
            out_specs=(hbm, hbm),
            scratch_shapes=[
                pltpu.SMEM((8, 128), jnp.int32),
                pltpu.VMEM((chan, nodes), BF16),
                dma((2 + steps,)),
            ],
            compiler_params=pltpu.CompilerParams(vmem_limit_bytes=4 << 20),
        )(*held)

    return jax.shard_map(
        on_device,
        mesh=mesh,
        in_specs=(
            P("tm", None, ("groups", "sensor")),
            P(("groups", "sensor"), None),
            P(("groups", "sensor")),
            P(("groups", "sensor"), None, None, None),
            P(),
            P(),
            P(),
            P(),
            P(),
            P(),
        ),
        out_specs=(P("tm", None, ("groups", "sensor")), P("tm", None, ("groups", "sensor"))),
        check_vma=False,
    )
```

```python
import functools

import jax
import jax.numpy as jnp
from jax import lax
from jax.experimental import pallas as pl
from jax.experimental.pallas import tpu as pltpu
from jax.sharding import PartitionSpec as P

CAP = 2
LAYERS = 2
HOPS = 2
UNROLL = 8
MESH = pl.DeviceIdType.MESH
F32 = jnp.float32
BF16 = jnp.bfloat16


def offsets_of(shards):
    found = []
    for step in (2, shards - 2, 1, shards - 1):
        step = step % shards
        if step and step not in found:
            found.append(step)
    return found


def order_of(steps):
    return list(range(steps - 2, -1, -2)) + list(range(steps - 1, -1, -2))


def body(
    shards,
    ranks,
    near_hbm,
    count_hbm,
    series_hbm,
    tiles_hbm,
    fgw_hbm,
    fgb_hbm,
    sw_hbm,
    sb_hbm,
    hmw_hbm,
    mb_hbm,
    outv,
    skipv,
    tiles_v,
    place_v,
    base_last,
    pool_last,
    near,
    count,
    tab_v,
    req_v,
    tab_r,
    src,
    series,
    fgw,
    fgb_row,
    sw,
    sb_row,
    hmw,
    mb_row,
    fgb,
    sb,
    mb,
    x1,
    edge0,
    edge1,
    fields,
    mid,
    base,
    hs,
    sendb,
    wg,
    wm,
    ws,
    tiles_sem,
    load_sem,
    series_sem,
    tab_send,
    tab_recv,
    place_sem,
    ready_sem,
    edge_send,
    edge_recv,
    usend,
    urecv,
    *pools,
):
    steps, chan, nodes = series.shape
    blocks, maxt, width = tiles_v.shape[0], tiles_v.shape[1], tiles_v.shape[2]
    offs = offsets_of(shards)
    order = order_of(steps)
    early = list(range(steps - 2, steps)) + list(range(steps - 2))
    me = lax.axis_index("sensor")
    tm = lax.axis_index("tm")
    peers = [lax.rem(me + off, shards) for off in offs]
    mirror = [offs.index(shards - off) for off in offs]
    after = lax.rem(tm + 1, ranks)
    before = lax.rem(tm + ranks - 1, ranks)
    dead = blocks + CAP * len(offs)
    last = LAYERS * HOPS * steps - 1

    def unit(layer, hop, t):
        return (layer * HOPS + hop) * steps + order.index(t)

    def pool_of(u):
        return pool_last if u == last else pools[u]

    def bounds(table, low):
        rel = table - low
        mine = (rel >= 0) & (rel < blocks)
        return rel, mine

    barrier = pltpu.get_barrier_semaphore()
    for peer in peers:
        pl.semaphore_signal(barrier, inc=1, device_id={"sensor": peer}, device_id_type=MESH)

    @pl.when(tm < ranks - 1)
    def _():
        pl.semaphore_signal(barrier, inc=1, device_id={"tm": after}, device_id_type=MESH)

    loads = [
        pltpu.make_async_copy(held, into, load_sem.at[i])
        for i, (held, into) in enumerate(
            (
                (near_hbm, near),
                (count_hbm, count),
                (fgw_hbm, fgw),
                (fgb_hbm, fgb_row),
                (hmw_hbm, hmw),
                (mb_hbm, mb_row),
                (sw_hbm, sw),
                (sb_hbm, sb_row),
            )
        )
    ]
    parts = [
        pltpu.make_async_copy(series_hbm.at[t], series.at[t], series_sem.at[t])
        for t in range(steps)
    ]
    soon = [order[0], order[0] - 1]
    for copy in loads[:2]:
        copy.start()
    for t in soon:
        parts[t].start()
    for copy in loads[2:6]:
        copy.start()
    for t in range(steps - 1, -1, -1):
        if t not in soon:
            parts[t].start()
    for copy in loads[6:]:
        copy.start()
    tiles_in = pltpu.make_async_copy(tiles_hbm, tiles_v, tiles_sem)

    loads[0].wait()
    loads[1].wait()
    slot = lax.broadcasted_iota(jnp.int32, near.shape, 0)
    tab_v[...] = jnp.full(tab_v.shape, -1, jnp.int32)
    table = jnp.where(slot < count[...], near[...], -1)
    tab_v[0:maxt, 0:blocks] = table
    upper = lax.broadcasted_iota(jnp.int32, req_v.shape[1:], 0) == 0
    leasts = []
    for o, peer in enumerate(peers):
        rel, mine = bounds(table, peer * blocks)
        least = jnp.min(jnp.where(mine, rel, blocks), axis=(0, 1), keepdims=True)
        most = jnp.max(jnp.where(mine, rel, -1), axis=(0, 1), keepdims=True)
        leasts.append(least)
        req_v[o] = jnp.where(upper, jnp.where(least < blocks, least, 0), jnp.maximum(most, 0))

    pl.semaphore_wait(barrier, len(peers) + jnp.where(tm > 0, 1, 0))

    @pl.when(tm > 0)
    def _():
        pl.semaphore_signal(ready_sem, inc=1, device_id={"tm": before}, device_id_type=MESH)

    tables = []
    for o, peer in enumerate(peers):
        copy = pltpu.make_async_remote_copy(
            src_ref=req_v.at[o],
            dst_ref=tab_r.at[mirror[o]],
            send_sem=tab_send.at[o],
            recv_sem=tab_recv.at[mirror[o]],
            device_id={"sensor": peer},
            device_id_type=MESH,
        )
        copy.start()
        tables.append(copy)

    for copy in loads[2:6]:
        copy.wait()

    def upright(row):
        tall = jnp.transpose(jnp.broadcast_to(row, (128, 128)))
        return jnp.concatenate([tall] * (width // 128), axis=1)

    def flipped(parts):
        return jnp.transpose(jnp.concatenate(parts, axis=0).astype(F32)).astype(BF16)

    both_mix = upright(jnp.concatenate([mb_row[pl.ds(i, 1), :] for i in range(LAYERS)], axis=1))
    for layer in range(LAYERS):
        mb[layer] = both_mix[layer * chan : (layer + 1) * chan]

    def prepare(layer):
        fgb[layer] = upright(fgb_row[pl.ds(layer, 1), :])
        wg[layer] = flipped([fgw[layer, 0], fgw[layer, 1]])
        w = hmw[layer]
        for i in range(3):
            wm[layer, i * chan : (i + 1) * chan] = w[:, (2 - i) * chan : (3 - i) * chan]

    prepare(0)
    for t in soon:
        parts[t].wait()

    def columns(b):
        return pl.ds(pl.multiple_of(b * width, width), width)

    def gate(layer, t):
        reach = 2**layer
        field = series if layer == 0 else x1
        u = unit(layer, 0, t)
        final = unit(layer, 1, t) == last

        def per_block(b, carry):
            cols = columns(b)
            cur = field[t, :, cols]
            if t >= reach:
                prev = field[t - reach, :, cols]
            else:
                held = edge0[:, cols] if layer == 0 else edge1[t, :, cols]
                prev = lax.select(tm > 0, held, jnp.zeros_like(held))
            both = jnp.concatenate([prev, cur], axis=0)
            pre = jnp.dot(wg[layer], both, preferred_element_type=F32) + fgb[layer]
            half = pre.shape[0] // 2
            h = jnp.tanh(pre[:half]) * (0.5 * jnp.tanh(0.5 * pre[half:]) + 0.5)
            h = h.astype(BF16)
            hs[t, b, layer * chan : (layer + 1) * chan] = h
            three = jnp.dot(wm[layer], h, preferred_element_type=F32)
            v = three[0:chan].astype(BF16)
            fields[t, b] = v
            pool_of(u)[b] = v
            mid[t, b] = three[chan : 2 * chan]
            rest = cur.astype(F32) + (three[2 * chan : 3 * chan] + mb[layer])
            if final:
                base_last[b] = rest
            else:
                base[t, b] = rest
            return carry

        lax.fori_loop(0, blocks, per_block, 0, unroll=UNROLL)

    def moves(layer, hop, t):
        u = unit(layer, hop, t)
        return [
            pltpu.make_async_remote_copy(
                src_ref=sendb.at[u, o],
                dst_ref=pool_of(u).at[pl.ds(blocks + CAP * mirror[o], CAP)],
                send_sem=usend.at[u, o],
                recv_sem=urecv.at[u, mirror[o]],
                device_id={"sensor": peer},
                device_id_type=MESH,
            )
            for o, peer in enumerate(peers)
        ]

    def arrive(layer, hop, t):
        u = unit(layer, hop, t)
        for o, peer in enumerate(peers):
            pltpu.make_async_remote_copy(
                src_ref=sendb.at[u, o],
                dst_ref=pool_of(u).at[pl.ds(blocks + CAP * o, CAP)],
                send_sem=usend.at[u, o],
                recv_sem=urecv.at[u, o],
                device_id={"sensor": peer},
                device_id_type=MESH,
            ).wait_recv()

    def send(layer, hop, t):
        u = unit(layer, hop, t)
        copies = moves(layer, hop, t)
        for o in range(len(peers)):
            for s in range(CAP):
                sendb[u, o, s] = fields[t, want[o][s]]
            copies[o].start()

    def diffuse(layer, hop, t):
        u = unit(layer, hop, t)

        def per_block(b, carry):
            picked = [pool_of(u)[src[k, b]] for k in range(maxt)]
            stack = jnp.concatenate(picked, axis=1)
            held = tiles_v[b].reshape(maxt * width, width)
            total = jnp.dot(stack, held, preferred_element_type=F32)
            if hop == 0:
                a = (mid[t, b] + total).astype(BF16)
                fields[t, b] = a
                pool_of(unit(layer, 1, t))[b] = a
            else:
                nxt = (base[t, b] + total).astype(BF16)
                into = x1 if layer == 0 else outv
                into[t, :, columns(b)] = nxt
            return carry

        lax.fori_loop(0, blocks, per_block, 0, unroll=UNROLL)

    def skip(t):
        def per_block(b, carry):
            out = jnp.dot(ws[...], hs[t, b], preferred_element_type=F32) + sb[...]
            skipv[t, :, columns(b)] = out.astype(BF16)
            return carry

        lax.fori_loop(0, blocks, per_block, 0, unroll=UNROLL)

    gate(0, order[0])

    want = []
    for o, peer in enumerate(peers):
        pltpu.make_async_remote_copy(
            src_ref=req_v.at[o],
            dst_ref=tab_r.at[o],
            send_sem=tab_send.at[o],
            recv_sem=tab_recv.at[o],
            device_id={"sensor": peer},
            device_id_type=MESH,
        ).wait_recv()
        asked = tab_r[o]
        want.append((asked[0, 0], asked[1, 0]))

    send(0, 0, order[0])
    parts[steps - 1].wait()
    first_edge = pltpu.make_async_remote_copy(
        src_ref=series.at[steps - 1],
        dst_ref=edge0,
        send_sem=edge_send.at[0],
        recv_sem=edge_recv.at[0],
        device_id={"tm": after},
        device_id_type=MESH,
    )

    @pl.when(tm < ranks - 1)
    def _():
        pl.semaphore_wait(ready_sem, 1)
        first_edge.start()

    tiles_in.start()
    for t in range(steps):
        if t != steps - 1 and t not in soon:
            parts[t].wait()
    for copy in loads[6:]:
        copy.wait()
    later_edges = [
        pltpu.make_async_remote_copy(
            src_ref=x1.at[steps - 2 + i],
            dst_ref=edge1.at[i],
            send_sem=edge_send.at[1 + i],
            recv_sem=edge_recv.at[1 + i],
            device_id={"tm": after},
            device_id_type=MESH,
        )
        for i in range(2)
    ]

    table = tab_v[...]
    rel, mine = bounds(table, me * blocks)
    place = jnp.where(mine, rel, dead)
    for o, peer in enumerate(peers):
        rel, mine = bounds(table, peer * blocks)
        place = jnp.where(mine, blocks + CAP * o + jnp.where(rel == leasts[o], 0, 1), place)
    place_v[...] = place
    places = pltpu.make_async_copy(place_v, src, place_sem)
    places.start()

    for t in early[1:]:
        if t == 0:
            pl.when(tm > 0)(first_edge.wait_recv)
        gate(0, t)
        send(0, 0, t)

    for u in range(last + 1):
        pool_of(u)[dead] = jnp.zeros((chan, width), BF16)
    for layer in range(1, LAYERS):
        prepare(layer)
    ws[...] = flipped([sw[layer] for layer in range(LAYERS)])
    row = sb_row[0:1, :]
    for layer in range(1, LAYERS):
        row = row + sb_row[pl.ds(layer, 1), :]
    for at in range(0, row.shape[1], 128):
        sb[at : at + 128] = upright(row[:, at : at + 128])

    places.wait()
    tiles_in.wait()
    done, sent = [], 0
    for t in early:
        arrive(0, 0, t)
        diffuse(0, 0, t)
        done.append(t)
        while sent < steps and order[sent] in done:
            send(0, 1, order[sent])
            sent += 1
    for t in order:
        arrive(0, 1, t)
        diffuse(0, 1, t)
        if t >= steps - 2:
            pl.when(tm < ranks - 1)(later_edges[t - (steps - 2)].start)
        else:
            gate(1, t + 2)
            send(1, 0, t + 2)
        if t < 2:
            pl.when(tm > 0)(later_edges[t].wait_recv)
            gate(1, t)
            send(1, 0, t)
    for t in order:
        skip(t)
    for t in order:
        arrive(1, 0, t)
        diffuse(1, 0, t)
        send(1, 1, t)
    for t in order[:-1]:
        arrive(1, 1, t)
        diffuse(1, 1, t)

    for copy in tables:
        copy.wait_send()

    @pl.when(tm < ranks - 1)
    def _():
        first_edge.wait_send()
        for copy in later_edges:
            copy.wait_send()

    for layer in range(LAYERS):
        for hop in range(HOPS):
            for t in order:
                if unit(layer, hop, t) != last:
                    for copy in moves(layer, hop, t):
                        copy.wait_send()
    arrive(1, 1, order[-1])
    for copy in moves(1, 1, order[-1]):
        copy.wait_send()


def finish(
    outv, skipv, tiles_v, place_v, base, pool, stream, skip_sum, src, tail, sems
):
    steps, chan, nodes = outv.shape
    blocks, maxt, width = tiles_v.shape[0], tiles_v.shape[1], tiles_v.shape[2]
    order = order_of(steps)
    places = pltpu.make_async_copy(place_v, src, sems.at[0])
    places.start()
    copies = [pltpu.make_async_copy(skipv, skip_sum, sems.at[1])]
    for i, t in enumerate(order[:-1]):
        copies.append(pltpu.make_async_copy(outv.at[t], stream.at[t], sems.at[2 + i]))
    for copy in copies:
        copy.start()
    places.wait()

    def per_block(b, carry):
        stack = jnp.concatenate([pool[src[k, b]] for k in range(maxt)], axis=1)
        held = tiles_v[b].reshape(maxt * width, width)
        total = jnp.dot(stack, held, preferred_element_type=F32)
        cols = pl.ds(pl.multiple_of(b * width, width), width)
        tail[:, cols] = (base[b] + total).astype(BF16)
        return carry

    lax.fori_loop(0, blocks, per_block, 0, unroll=UNROLL)
    final = pltpu.make_async_copy(tail, stream.at[order[-1]], sems.at[1 + steps])
    final.start()
    for copy in copies:
        copy.wait()
    final.wait()


def solution(mesh):
    shards, ranks = mesh.shape["sensor"], mesh.shape["tm"]
    links = len(offsets_of(shards))

    def on_device(
        series, neighbours, tile_count, tiles, fgw, fgb, skip_weight, skip_b, hop_mixing, mix_b
    ):
        steps, chan, nodes = series.shape
        blocks, maxt, width = tiles.shape[0], tiles.shape[1], tiles.shape[2]
        wide = skip_weight.shape[1]
        pool = blocks + CAP * links + 1
        units = LAYERS * HOPS * steps
        fgw_t = jnp.swapaxes(fgw, 2, 3)
        skip_t = jnp.swapaxes(skip_weight, 1, 2)
        operands = [
            pltpu.with_memory_space_constraint(held, pltpu.HBM)
            for held in (
                neighbours.T,
                tile_count[None, :],
                series,
                tiles,
                fgw_t,
                fgb,
                skip_t,
                skip_b,
                hop_mixing,
                mix_b,
            )
        ]
        vmem = pl.BlockSpec(memory_space=pltpu.VMEM)
        hbm = pl.BlockSpec(memory_space=pltpu.HBM)
        dma = pltpu.SemaphoreType.DMA
        results = (
            jax.ShapeDtypeStruct(series.shape, BF16),
            jax.ShapeDtypeStruct((steps, wide, nodes), BF16),
        )
        held = pl.pallas_call(
            functools.partial(body, shards, ranks),
            out_shape=results
            + (
                jax.ShapeDtypeStruct(tiles.shape, BF16),
                jax.ShapeDtypeStruct((8, 128), jnp.int32),
                jax.ShapeDtypeStruct((blocks, chan, width), F32),
                jax.ShapeDtypeStruct((pool, chan, width), BF16),
            ),
            in_specs=[hbm] * 10,
            out_specs=(vmem,) * 6,
            scratch_shapes=[
                pltpu.VMEM((maxt, blocks), jnp.int32),
                pltpu.VMEM((1, blocks), jnp.int32),
                pltpu.VMEM((8, 128), jnp.int32),
                pltpu.VMEM((links, 8, 128), jnp.int32),
                pltpu.VMEM((links, 8, 128), jnp.int32),
                pltpu.SMEM((8, 128), jnp.int32),
                pltpu.VMEM(series.shape, BF16),
                pltpu.VMEM(fgw_t.shape, BF16),
                pltpu.VMEM(fgb.shape, F32),
                pltpu.VMEM(skip_t.shape, BF16),
                pltpu.VMEM(skip_b.shape, F32),
                pltpu.VMEM(hop_mixing.shape, BF16),
                pltpu.VMEM(mix_b.shape, F32),
                pltpu.VMEM((LAYERS, 2 * chan, width), F32),
                pltpu.VMEM((wide, width), F32),
                pltpu.VMEM((LAYERS, chan, width), F32),
                pltpu.VMEM(series.shape, BF16),
                pltpu.VMEM((chan, nodes), BF16),
                pltpu.VMEM((2, chan, nodes), BF16),
                pltpu.VMEM((steps, blocks, chan, width), BF16),
                pltpu.VMEM((steps, blocks, chan, width), F32),
                pltpu.VMEM((steps, blocks, chan, width), F32),
                pltpu.VMEM((steps, blocks, LAYERS * chan, width), BF16),
                pltpu.VMEM((units, links, CAP, chan, width), BF16),
                pltpu.VMEM((LAYERS, 2 * chan, 2 * chan), BF16),
                pltpu.VMEM((LAYERS, 3 * chan, chan), BF16),
                pltpu.VMEM((wide, LAYERS * chan), BF16),
                dma,
                dma((8,)),
                dma((steps,)),
                dma((links,)),
                dma((links,)),
                dma,
                pltpu.SemaphoreType.REGULAR,
                dma((3,)),
                dma((3,)),
                dma((units, links)),
                dma((units, links)),
            ]
            + [pltpu.VMEM((pool, chan, width), BF16)] * (units - 1),
            compiler_params=pltpu.CompilerParams(
                collective_id=0, has_side_effects=True, vmem_limit_bytes=40 << 20
            ),
        )(*operands)
        return pl.pallas_call(
            finish,
            out_shape=results,
            in_specs=[vmem] * 6,
            out_specs=(hbm, hbm),
            scratch_shapes=[
                pltpu.SMEM((8, 128), jnp.int32),
                pltpu.VMEM((chan, nodes), BF16),
                dma((2 + steps,)),
            ],
            compiler_params=pltpu.CompilerParams(vmem_limit_bytes=4 << 20),
        )(*held)

    return jax.shard_map(
        on_device,
        mesh=mesh,
        in_specs=(
            P("tm", None, ("groups", "sensor")),
            P(("groups", "sensor"), None),
            P(("groups", "sensor")),
            P(("groups", "sensor"), None, None, None),
            P(),
            P(),
            P(),
            P(),
            P(),
            P(),
        ),
        out_specs=(P("tm", None, ("groups", "sensor")), P("tm", None, ("groups", "sensor"))),
        check_vma=False,
    )
```

```python
import functools

import jax
import jax.numpy as jnp
from jax import lax
from jax.experimental import pallas as pl
from jax.experimental.pallas import tpu as pltpu
from jax.sharding import PartitionSpec as P

CAP = 2
LAYERS = 2
HOPS = 2
UNROLL = 8
MESH = pl.DeviceIdType.MESH
F32 = jnp.float32
BF16 = jnp.bfloat16


def offsets_of(shards):
    found = []
    for step in (2, shards - 2, 1, shards - 1):
        step = step % shards
        if step and step not in found:
            found.append(step)
    return found


def order_of(steps):
    return list(range(steps - 1, -1, -2)) + list(range(steps - 2, -1, -2))


def body(
    shards,
    ranks,
    near_hbm,
    count_hbm,
    series_hbm,
    tiles_hbm,
    fgw_hbm,
    fgb_hbm,
    sw_hbm,
    sb_hbm,
    hmw_hbm,
    mb_hbm,
    outv,
    skipv,
    tiles_v,
    place_v,
    base_last,
    pool_last,
    near,
    count,
    tab_v,
    req_v,
    tab_r,
    src,
    series,
    fgw,
    fgb_row,
    sw,
    sb_row,
    hmw,
    mb_row,
    fgb,
    sb,
    mb,
    x1,
    edge0,
    edge1,
    fields,
    mid,
    base,
    hs,
    sendb,
    wg,
    wm,
    ws,
    tiles_sem,
    load_sem,
    series_sem,
    tab_send,
    tab_recv,
    place_sem,
    ready_sem,
    here_sem,
    edge_send,
    edge_recv,
    usend,
    urecv,
    *pools,
):
    steps, chan, nodes = series.shape
    blocks, maxt, width = tiles_v.shape[0], tiles_v.shape[1], tiles_v.shape[2]
    offs = offsets_of(shards)
    order = order_of(steps)
    early = list(range(steps - 1, -1, -1))
    me = lax.axis_index("sensor")
    tm = lax.axis_index("tm")
    peers = [lax.rem(me + off, shards) for off in offs]
    mirror = [offs.index(shards - off) for off in offs]
    after = lax.rem(tm + 1, ranks)
    before = lax.rem(tm + ranks - 1, ranks)
    even = lax.rem(tm, 2) == 0
    odd = jnp.logical_not(even)
    above, below = tm < ranks - 1, tm > 0
    dead = blocks + CAP * len(offs)
    last = LAYERS * HOPS * steps - 1

    def unit(layer, hop, t):
        return (layer * HOPS + hop) * steps + order.index(t)

    def pool_of(u):
        return pool_last if u == last else pools[u]

    def bounds(table, low):
        rel = table - low
        mine = (rel >= 0) & (rel < blocks)
        return rel, mine

    barrier = pltpu.get_barrier_semaphore()
    for peer in peers:

        @pl.when(peer > me)
        def _():
            pl.semaphore_signal(barrier, inc=1, device_id={"sensor": peer}, device_id_type=MESH)


    @pl.when(odd & above)
    def _():
        pl.semaphore_signal(barrier, inc=1, device_id={"tm": after}, device_id_type=MESH)

    @pl.when(odd & below)
    def _():
        pl.semaphore_signal(barrier, inc=1, device_id={"tm": before}, device_id_type=MESH)

    loads = [
        pltpu.make_async_copy(held, into, load_sem.at[i])
        for i, (held, into) in enumerate(
            (
                (near_hbm, near),
                (count_hbm, count),
                (fgw_hbm, fgw),
                (fgb_hbm, fgb_row),
                (hmw_hbm, hmw),
                (mb_hbm, mb_row),
                (sw_hbm, sw),
                (sb_hbm, sb_row),
            )
        )
    ]
    parts = [
        pltpu.make_async_copy(series_hbm.at[t], series.at[t], series_sem.at[t])
        for t in range(steps)
    ]
    soon = [early[0], early[0] - 1]
    for copy in loads[:2]:
        copy.start()
    for t in soon:
        parts[t].start()
    for copy in loads[2:6]:
        copy.start()
    for t in range(steps - 1, -1, -1):
        if t not in soon:
            parts[t].start()
    for copy in loads[6:]:
        copy.start()
    tiles_in = pltpu.make_async_copy(tiles_hbm, tiles_v, tiles_sem)

    lower = sum([jnp.where(peer < me, 1, 0) for peer in peers])
    beside = jnp.where(above, 1, 0) + jnp.where(below, 1, 0)
    greeted = lower + jnp.where(even, beside, 0)

    @pl.when(greeted > 0)
    def _():
        pl.semaphore_wait(barrier, greeted)

    for o, peer in enumerate(peers):

        @pl.when(peer < me)
        def _():
            pl.semaphore_signal(
                here_sem.at[mirror[o]], inc=1, device_id={"sensor": peer}, device_id_type=MESH
            )

    @pl.when(even & below)
    def _():
        pl.semaphore_signal(ready_sem, inc=1, device_id={"tm": before}, device_id_type=MESH)

    loads[0].wait()
    loads[1].wait()
    slot = lax.broadcasted_iota(jnp.int32, near.shape, 0)
    tab_v[...] = jnp.full(tab_v.shape, -1, jnp.int32)
    table = jnp.where(slot < count[...], near[...], -1)
    tab_v[0:maxt, 0:blocks] = table
    line = lax.broadcasted_iota(jnp.int32, req_v.shape, 0)
    leasts, asks = [], jnp.zeros(req_v.shape, jnp.int32)
    for o, peer in enumerate(peers):
        rel, mine = bounds(table, peer * blocks)
        least = jnp.min(jnp.where(mine, rel, blocks), axis=(0, 1), keepdims=True)
        most = jnp.max(jnp.where(mine, rel, -1), axis=(0, 1), keepdims=True)
        leasts.append(least)
        asks = jnp.where(line == CAP * o, jnp.where(least < blocks, least, 0), asks)
        asks = jnp.where(line == CAP * o + 1, jnp.maximum(most, 0), asks)
    req_v[...] = asks

    tables = [
        pltpu.make_async_remote_copy(
            src_ref=req_v,
            dst_ref=tab_r.at[mirror[o]],
            send_sem=tab_send.at[o],
            recv_sem=tab_recv.at[mirror[o]],
            device_id={"sensor": peer},
            device_id_type=MESH,
        )
        for o, peer in enumerate(peers)
    ]
    for o, peer in enumerate(peers):
        pl.when(peer < me)(tables[o].start)

    for copy in loads[2:6]:
        copy.wait()

    def upright(row):
        tall = jnp.transpose(jnp.broadcast_to(row, (128, 128)))
        return jnp.concatenate([tall] * (width // 128), axis=1)

    def flipped(parts):
        return jnp.transpose(jnp.concatenate(parts, axis=0).astype(F32)).astype(BF16)

    both_mix = upright(jnp.concatenate([mb_row[pl.ds(i, 1), :] for i in range(LAYERS)], axis=1))
    for layer in range(LAYERS):
        mb[layer] = both_mix[layer * chan : (layer + 1) * chan]

    def prepare(layer):
        fgb[layer] = upright(fgb_row[pl.ds(layer, 1), :])
        wg[layer] = flipped([fgw[layer, 0], fgw[layer, 1]])
        w = hmw[layer]
        for i in range(3):
            wm[layer, i * chan : (i + 1) * chan] = w[:, (2 - i) * chan : (3 - i) * chan]

    prepare(0)
    for t in soon:
        parts[t].wait()

    def columns(b):
        return pl.ds(pl.multiple_of(b * width, width), width)

    def gate(layer, t):
        reach = 2**layer
        field = series if layer == 0 else x1
        u = unit(layer, 0, t)
        final = unit(layer, 1, t) == last

        def per_block(b, carry):
            cols = columns(b)
            cur = field[t, :, cols]
            if t >= reach:
                prev = field[t - reach, :, cols]
            else:
                held = edge0[:, cols] if layer == 0 else edge1[t, :, cols]
                prev = lax.select(below, held, jnp.zeros_like(held))
            both = jnp.concatenate([prev, cur], axis=0)
            pre = jnp.dot(wg[layer], both, preferred_element_type=F32) + fgb[layer]
            half = pre.shape[0] // 2
            h = jnp.tanh(pre[:half]) * (0.5 * jnp.tanh(0.5 * pre[half:]) + 0.5)
            h = h.astype(BF16)
            hs[t, b, layer * chan : (layer + 1) * chan] = h
            three = jnp.dot(wm[layer], h, preferred_element_type=F32)
            v = three[0:chan].astype(BF16)
            fields[t, b] = v
            pool_of(u)[b] = v
            mid[t, b] = three[chan : 2 * chan]
            rest = cur.astype(F32) + (three[2 * chan : 3 * chan] + mb[layer])
            if final:
                base_last[b] = rest
            else:
                base[t, b] = rest
            return carry

        lax.fori_loop(0, blocks, per_block, 0, unroll=UNROLL)

    def moves(layer, hop, t):
        u = unit(layer, hop, t)
        return [
            pltpu.make_async_remote_copy(
                src_ref=sendb.at[u, o],
                dst_ref=pool_of(u).at[pl.ds(blocks + CAP * mirror[o], CAP)],
                send_sem=usend.at[u, o],
                recv_sem=urecv.at[u, mirror[o]],
                device_id={"sensor": peer},
                device_id_type=MESH,
            )
            for o, peer in enumerate(peers)
        ]

    def arrive(layer, hop, t):
        u = unit(layer, hop, t)
        for o, peer in enumerate(peers):
            copy = pltpu.make_async_remote_copy(
                src_ref=sendb.at[u, o],
                dst_ref=pool_of(u).at[pl.ds(blocks + CAP * o, CAP)],
                send_sem=usend.at[u, o],
                recv_sem=urecv.at[u, o],
                device_id={"sensor": peer},
                device_id_type=MESH,
            )
            copy.wait_recv()

    def send(layer, hop, t):
        u = unit(layer, hop, t)
        copies = moves(layer, hop, t)
        for o in range(len(peers)):
            for s in range(CAP):
                sendb[u, o, s] = fields[t, want[o][s]]
            copies[o].start()

    def diffuse(layer, hop, t):
        u = unit(layer, hop, t)

        def per_block(b, carry):
            picked = [pool_of(u)[src[k, b]] for k in range(maxt)]
            stack = jnp.concatenate(picked, axis=1)
            held = tiles_v[b].reshape(maxt * width, width)
            total = jnp.dot(stack, held, preferred_element_type=F32)
            if hop == 0:
                a = (mid[t, b] + total).astype(BF16)
                fields[t, b] = a
                pool_of(unit(layer, 1, t))[b] = a
            else:
                nxt = (base[t, b] + total).astype(BF16)
                into = x1 if layer == 0 else outv
                into[t, :, columns(b)] = nxt
            return carry

        lax.fori_loop(0, blocks, per_block, 0, unroll=UNROLL)

    def skip(t):
        def per_block(b, carry):
            out = jnp.dot(ws[...], hs[t, b], preferred_element_type=F32) + sb[...]
            skipv[t, :, columns(b)] = out.astype(BF16)
            return carry

        lax.fori_loop(0, blocks, per_block, 0, unroll=UNROLL)

    gate(0, early[0])

    first = unit(0, 0, early[0])

    def greet(final):
        for o, peer in enumerate(peers):

            @pl.when((peer > me) & ((peer == shards - 1) == final))
            def _():
                pl.semaphore_wait(here_sem.at[o], 1)
                tables[o].start()

    def wanted(o):
        asked = tab_r[o]
        row = CAP * mirror[o]
        return asked[row, 0], asked[row + 1, 0]

    def serve(final):
        copies = moves(0, 0, early[0])
        for o, peer in enumerate(peers):

            @pl.when((peer == shards - 1) == final)
            def _():
                pltpu.make_async_remote_copy(
                    src_ref=req_v,
                    dst_ref=tab_r.at[o],
                    send_sem=tab_send.at[o],
                    recv_sem=tab_recv.at[o],
                    device_id={"sensor": peer},
                    device_id_type=MESH,
                ).wait_recv()

                for s, block in enumerate(wanted(o)):
                    sendb[first, o, s] = fields[early[0], block]
                copies[o].start()

    greet(False)
    greet(True)
    serve(False)
    serve(True)
    want = [wanted(o) for o in range(len(peers))]
    first_edge = pltpu.make_async_remote_copy(
        src_ref=series.at[steps - 1],
        dst_ref=edge0,
        send_sem=edge_send.at[0],
        recv_sem=edge_recv.at[0],
        device_id={"tm": after},
        device_id_type=MESH,
    )
    tiles_in.start()
    for t in range(steps):
        if t not in soon:
            parts[t].wait()
    for copy in loads[6:]:
        copy.wait()
    later_edges = [
        pltpu.make_async_remote_copy(
            src_ref=x1.at[steps - 2 + i],
            dst_ref=edge1.at[i],
            send_sem=edge_send.at[1 + i],
            recv_sem=edge_recv.at[1 + i],
            device_id={"tm": after},
            device_id_type=MESH,
        )
        for i in range(2)
    ]

    table = tab_v[...]
    rel, mine = bounds(table, me * blocks)
    place = jnp.where(mine, rel, dead)
    for o, peer in enumerate(peers):
        rel, mine = bounds(table, peer * blocks)
        place = jnp.where(mine, blocks + CAP * o + jnp.where(rel == leasts[o], 0, 1), place)
    place_v[...] = place
    places = pltpu.make_async_copy(place_v, src, place_sem)
    places.start()

    for t in early[1:]:
        if t == 0:

            @pl.when(odd & above)
            def _():
                pl.semaphore_wait(ready_sem, 1)

            pl.when(above)(first_edge.start)
            pl.when(below)(first_edge.wait_recv)
        gate(0, t)
        send(0, 0, t)

    for u in range(last + 1):
        pool_of(u)[dead] = jnp.zeros((chan, width), BF16)
    for layer in range(1, LAYERS):
        prepare(layer)
    ws[...] = flipped([sw[layer] for layer in range(LAYERS)])
    row = sb_row[0:1, :]
    for layer in range(1, LAYERS):
        row = row + sb_row[pl.ds(layer, 1), :]
    for at in range(0, row.shape[1], 128):
        sb[at : at + 128] = upright(row[:, at : at + 128])

    places.wait()
    tiles_in.wait()
    done, sent = [], 0
    for t in early:
        arrive(0, 0, t)
        diffuse(0, 0, t)
        done.append(t)
        while sent < steps and order[sent] in done:
            send(0, 1, order[sent])
            sent += 1
    for t in order:
        arrive(0, 1, t)
        diffuse(0, 1, t)
        if t >= steps - 2:
            pl.when(above)(later_edges[t - (steps - 2)].start)
        else:
            gate(1, t + 2)
            send(1, 0, t + 2)
        if t < 2:
            pl.when(below)(later_edges[t].wait_recv)
            gate(1, t)
            send(1, 0, t)
    for t in order:
        skip(t)
    for t in order:
        arrive(1, 0, t)
        diffuse(1, 0, t)
        send(1, 1, t)
    for t in order[:-1]:
        arrive(1, 1, t)
        diffuse(1, 1, t)

    for copy in tables:
        copy.wait_send()

    @pl.when(above)
    def _():
        first_edge.wait_send()
        for copy in later_edges:
            copy.wait_send()

    for layer in range(LAYERS):
        for hop in range(HOPS):
            for t in order:
                u = unit(layer, hop, t)
                if u != last:
                    for copy in moves(layer, hop, t):
                        copy.wait_send()
    arrive(1, 1, order[-1])
    for copy in moves(1, 1, order[-1]):
        copy.wait_send()


def finish(
    outv, skipv, tiles_v, place_v, base, pool, stream, skip_sum, src, tail, sems
):
    steps, chan, nodes = outv.shape
    blocks, maxt, width = tiles_v.shape[0], tiles_v.shape[1], tiles_v.shape[2]
    order = order_of(steps)
    places = pltpu.make_async_copy(place_v, src, sems.at[0])
    places.start()
    copies = [pltpu.make_async_copy(skipv, skip_sum, sems.at[1])]
    for i, t in enumerate(order[:-1]):
        copies.append(pltpu.make_async_copy(outv.at[t], stream.at[t], sems.at[2 + i]))
    for copy in copies:
        copy.start()
    places.wait()

    def per_block(b, carry):
        stack = jnp.concatenate([pool[src[k, b]] for k in range(maxt)], axis=1)
        held = tiles_v[b].reshape(maxt * width, width)
        total = jnp.dot(stack, held, preferred_element_type=F32)
        cols = pl.ds(pl.multiple_of(b * width, width), width)
        tail[:, cols] = (base[b] + total).astype(BF16)
        return carry

    lax.fori_loop(0, blocks, per_block, 0, unroll=UNROLL)
    final = pltpu.make_async_copy(tail, stream.at[order[-1]], sems.at[1 + steps])
    final.start()
    for copy in copies:
        copy.wait()
    final.wait()


def solution(mesh):
    shards, ranks = mesh.shape["sensor"], mesh.shape["tm"]
    links = len(offsets_of(shards))

    def on_device(
        series, neighbours, tile_count, tiles, fgw, fgb, skip_weight, skip_b, hop_mixing, mix_b
    ):
        steps, chan, nodes = series.shape
        blocks, maxt, width = tiles.shape[0], tiles.shape[1], tiles.shape[2]
        wide = skip_weight.shape[1]
        pool = blocks + CAP * links + 1
        units = LAYERS * HOPS * steps
        fgw_t = jnp.swapaxes(fgw, 2, 3)
        skip_t = jnp.swapaxes(skip_weight, 1, 2)
        operands = [
            pltpu.with_memory_space_constraint(held, pltpu.HBM)
            for held in (
                neighbours.T,
                tile_count[None, :],
                series,
                tiles,
                fgw_t,
                fgb,
                skip_t,
                skip_b,
                hop_mixing,
                mix_b,
            )
        ]
        vmem = pl.BlockSpec(memory_space=pltpu.VMEM)
        hbm = pl.BlockSpec(memory_space=pltpu.HBM)
        dma = pltpu.SemaphoreType.DMA
        results = (
            jax.ShapeDtypeStruct(series.shape, BF16),
            jax.ShapeDtypeStruct((steps, wide, nodes), BF16),
        )
        held = pl.pallas_call(
            functools.partial(body, shards, ranks),
            out_shape=results
            + (
                jax.ShapeDtypeStruct(tiles.shape, BF16),
                jax.ShapeDtypeStruct((8, 128), jnp.int32),
                jax.ShapeDtypeStruct((blocks, chan, width), F32),
                jax.ShapeDtypeStruct((pool, chan, width), BF16),
            ),
            in_specs=[hbm] * 10,
            out_specs=(vmem,) * 6,
            scratch_shapes=[
                pltpu.VMEM((maxt, blocks), jnp.int32),
                pltpu.VMEM((1, blocks), jnp.int32),
                pltpu.VMEM((8, 128), jnp.int32),
                pltpu.VMEM((8, 128), jnp.int32),
                pltpu.VMEM((links, 8, 128), jnp.int32),
                pltpu.SMEM((8, 128), jnp.int32),
                pltpu.VMEM(series.shape, BF16),
                pltpu.VMEM(fgw_t.shape, BF16),
                pltpu.VMEM(fgb.shape, F32),
                pltpu.VMEM(skip_t.shape, BF16),
                pltpu.VMEM(skip_b.shape, F32),
                pltpu.VMEM(hop_mixing.shape, BF16),
                pltpu.VMEM(mix_b.shape, F32),
                pltpu.VMEM((LAYERS, 2 * chan, width), F32),
                pltpu.VMEM((wide, width), F32),
                pltpu.VMEM((LAYERS, chan, width), F32),
                pltpu.VMEM(series.shape, BF16),
                pltpu.VMEM((chan, nodes), BF16),
                pltpu.VMEM((2, chan, nodes), BF16),
                pltpu.VMEM((steps, blocks, chan, width), BF16),
                pltpu.VMEM((steps, blocks, chan, width), F32),
                pltpu.VMEM((steps, blocks, chan, width), F32),
                pltpu.VMEM((steps, blocks, LAYERS * chan, width), BF16),
                pltpu.VMEM((units, links, CAP, chan, width), BF16),
                pltpu.VMEM((LAYERS, 2 * chan, 2 * chan), BF16),
                pltpu.VMEM((LAYERS, 3 * chan, chan), BF16),
                pltpu.VMEM((wide, LAYERS * chan), BF16),
                dma,
                dma((8,)),
                dma((steps,)),
                dma((links,)),
                dma((links,)),
                dma,
                pltpu.SemaphoreType.REGULAR,
                pltpu.SemaphoreType.REGULAR((links,)),
                dma((3,)),
                dma((3,)),
                dma((units, links)),
                dma((units, links)),
            ]
            + [pltpu.VMEM((pool, chan, width), BF16)] * (units - 1),
            compiler_params=pltpu.CompilerParams(
                collective_id=0, has_side_effects=True, vmem_limit_bytes=40 << 20
            ),
        )(*operands)
        return pl.pallas_call(
            finish,
            out_shape=results,
            in_specs=[vmem] * 6,
            out_specs=(hbm, hbm),
            scratch_shapes=[
                pltpu.SMEM((8, 128), jnp.int32),
                pltpu.VMEM((chan, nodes), BF16),
                dma((2 + steps,)),
            ],
            compiler_params=pltpu.CompilerParams(vmem_limit_bytes=4 << 20),
        )(*held)

    return jax.shard_map(
        on_device,
        mesh=mesh,
        in_specs=(
            P("tm", None, ("groups", "sensor")),
            P(("groups", "sensor"), None),
            P(("groups", "sensor")),
            P(("groups", "sensor"), None, None, None),
            P(),
            P(),
            P(),
            P(),
            P(),
            P(),
        ),
        out_specs=(P("tm", None, ("groups", "sensor")), P("tm", None, ("groups", "sensor"))),
        check_vma=False,
    )
```

```python
import functools

import jax
import jax.numpy as jnp
from jax import lax
from jax.experimental import pallas as pl
from jax.experimental.pallas import tpu as pltpu
from jax.sharding import PartitionSpec as P

CAP = 2
LAYERS = 2
HOPS = 2
UNROLL = 8
MESH = pl.DeviceIdType.MESH
F32 = jnp.float32
BF16 = jnp.bfloat16


def offsets_of(shards):
    found = []
    for step in (2, shards - 2, 1, shards - 1):
        step = step % shards
        if step and step not in found:
            found.append(step)
    return found


def order_of(steps):
    return list(range(steps - 1, -1, -2)) + list(range(steps - 2, -1, -2))


def body(
    shards,
    ranks,
    near_hbm,
    count_hbm,
    series_hbm,
    tiles_hbm,
    fgw_hbm,
    fgb_hbm,
    sw_hbm,
    sb_hbm,
    hmw_hbm,
    mb_hbm,
    outv,
    skipv,
    tiles_v,
    place_v,
    base_last,
    pool_last,
    near,
    count,
    tab_v,
    req_v,
    tab_r,
    src,
    series,
    fgw,
    fgb_row,
    sw,
    sb_row,
    hmw,
    mb_row,
    fgb,
    sb,
    mb,
    x1,
    edge0,
    edge1,
    fields,
    mid,
    base,
    hs,
    sendb,
    wg,
    wm,
    ws,
    tiles_sem,
    load_sem,
    series_sem,
    tab_send,
    tab_recv,
    place_sem,
    ready_sem,
    known_sem,
    relay_sem,
    here_sem,
    edge_send,
    edge_recv,
    usend,
    urecv,
    *pools,
):
    steps, chan, nodes = series.shape
    blocks, maxt, width = tiles_v.shape[0], tiles_v.shape[1], tiles_v.shape[2]
    offs = offsets_of(shards)
    order = order_of(steps)
    early = list(range(steps - 1, -1, -1))
    me = lax.axis_index("sensor")
    tm = lax.axis_index("tm")
    peers = [lax.rem(me + off, shards) for off in offs]
    mirror = [offs.index(shards - off) for off in offs]
    after = lax.rem(tm + 1, ranks)
    before = lax.rem(tm + ranks - 1, ranks)
    even = lax.rem(tm, 2) == 0
    odd = jnp.logical_not(even)
    via = shards == 4
    root = me == 0 if via else me >= 0
    above, below = tm < ranks - 1, tm > 0
    dead = blocks + CAP * len(offs)
    last = LAYERS * HOPS * steps - 1

    def unit(layer, hop, t):
        return (layer * HOPS + hop) * steps + order.index(t)

    def pool_of(u):
        return pool_last if u == last else pools[u]

    def bounds(table, low):
        rel = table - low
        mine = (rel >= 0) & (rel < blocks)
        return rel, mine

    barrier = pltpu.get_barrier_semaphore()
    for peer in peers:

        @pl.when(peer > me)
        def _():
            pl.semaphore_signal(barrier, inc=1, device_id={"sensor": peer}, device_id_type=MESH)


    @pl.when(root & odd & above)
    def _():
        pl.semaphore_signal(barrier, inc=1, device_id={"tm": after}, device_id_type=MESH)

    @pl.when(root & odd & below)
    def _():
        pl.semaphore_signal(barrier, inc=1, device_id={"tm": before}, device_id_type=MESH)

    loads = [
        pltpu.make_async_copy(held, into, load_sem.at[i])
        for i, (held, into) in enumerate(
            (
                (near_hbm, near),
                (count_hbm, count),
                (fgw_hbm, fgw),
                (fgb_hbm, fgb_row),
                (hmw_hbm, hmw),
                (mb_hbm, mb_row),
                (sw_hbm, sw),
                (sb_hbm, sb_row),
            )
        )
    ]
    parts = [
        pltpu.make_async_copy(series_hbm.at[t], series.at[t], series_sem.at[t])
        for t in range(steps)
    ]
    soon = [early[0], early[0] - 1]
    for copy in loads[:2]:
        copy.start()
    for t in soon:
        parts[t].start()
    for copy in loads[2:6]:
        copy.start()
    for t in range(steps - 1, -1, -1):
        if t not in soon:
            parts[t].start()
    for copy in loads[6:]:
        copy.start()
    tiles_in = pltpu.make_async_copy(tiles_hbm, tiles_v, tiles_sem)

    lower = sum([jnp.where(peer < me, 1, 0) for peer in peers])
    beside = jnp.where(above, 1, 0) + jnp.where(below, 1, 0)
    greeted = lower + jnp.where(root & even, beside, 0)

    @pl.when(greeted > 0)
    def _():
        pl.semaphore_wait(barrier, greeted)

    for o, peer in enumerate(peers):

        @pl.when(peer < me)
        def _():
            pl.semaphore_signal(
                here_sem.at[mirror[o]], inc=1, device_id={"sensor": peer}, device_id_type=MESH
            )

    @pl.when(root & even & below)
    def _():
        pl.semaphore_signal(ready_sem, inc=1, device_id={"tm": before}, device_id_type=MESH)

    if via:

        @pl.when(root & even & above)
        def _():
            pl.semaphore_signal(known_sem, inc=1, device_id={"tm": after}, device_id_type=MESH)

    loads[0].wait()
    loads[1].wait()
    slot = lax.broadcasted_iota(jnp.int32, near.shape, 0)
    tab_v[...] = jnp.full(tab_v.shape, -1, jnp.int32)
    table = jnp.where(slot < count[...], near[...], -1)
    tab_v[0:maxt, 0:blocks] = table
    line = lax.broadcasted_iota(jnp.int32, req_v.shape, 0)
    leasts, asks = [], jnp.zeros(req_v.shape, jnp.int32)
    for o, peer in enumerate(peers):
        rel, mine = bounds(table, peer * blocks)
        least = jnp.min(jnp.where(mine, rel, blocks), axis=(0, 1), keepdims=True)
        most = jnp.max(jnp.where(mine, rel, -1), axis=(0, 1), keepdims=True)
        leasts.append(least)
        asks = jnp.where(line == CAP * o, jnp.where(least < blocks, least, 0), asks)
        asks = jnp.where(line == CAP * o + 1, jnp.maximum(most, 0), asks)
    req_v[...] = asks

    tables = [
        pltpu.make_async_remote_copy(
            src_ref=req_v,
            dst_ref=tab_r.at[mirror[o]],
            send_sem=tab_send.at[o],
            recv_sem=tab_recv.at[mirror[o]],
            device_id={"sensor": peer},
            device_id_type=MESH,
        )
        for o, peer in enumerate(peers)
    ]
    for o, peer in enumerate(peers):
        pl.when(peer < me)(tables[o].start)

    for copy in loads[2:6]:
        copy.wait()

    def upright(row):
        tall = jnp.transpose(jnp.broadcast_to(row, (128, 128)))
        return jnp.concatenate([tall] * (width // 128), axis=1)

    def flipped(parts):
        return jnp.transpose(jnp.concatenate(parts, axis=0).astype(F32)).astype(BF16)

    both_mix = upright(jnp.concatenate([mb_row[pl.ds(i, 1), :] for i in range(LAYERS)], axis=1))
    for layer in range(LAYERS):
        mb[layer] = both_mix[layer * chan : (layer + 1) * chan]

    def prepare(layer):
        fgb[layer] = upright(fgb_row[pl.ds(layer, 1), :])
        wg[layer] = flipped([fgw[layer, 0], fgw[layer, 1]])
        w = hmw[layer]
        for i in range(3):
            wm[layer, i * chan : (i + 1) * chan] = w[:, (2 - i) * chan : (3 - i) * chan]

    prepare(0)
    for t in soon:
        parts[t].wait()

    def columns(b):
        return pl.ds(pl.multiple_of(b * width, width), width)

    def gate(layer, t):
        reach = 2**layer
        field = series if layer == 0 else x1
        u = unit(layer, 0, t)
        final = unit(layer, 1, t) == last

        def per_block(b, carry):
            cols = columns(b)
            cur = field[t, :, cols]
            if t >= reach:
                prev = field[t - reach, :, cols]
            else:
                held = edge0[:, cols] if layer == 0 else edge1[t, :, cols]
                prev = lax.select(below, held, jnp.zeros_like(held))
            both = jnp.concatenate([prev, cur], axis=0)
            pre = jnp.dot(wg[layer], both, preferred_element_type=F32) + fgb[layer]
            half = pre.shape[0] // 2
            h = jnp.tanh(pre[:half]) * (0.5 * jnp.tanh(0.5 * pre[half:]) + 0.5)
            h = h.astype(BF16)
            hs[t, b, layer * chan : (layer + 1) * chan] = h
            three = jnp.dot(wm[layer], h, preferred_element_type=F32)
            v = three[0:chan].astype(BF16)
            fields[t, b] = v
            pool_of(u)[b] = v
            mid[t, b] = three[chan : 2 * chan]
            rest = cur.astype(F32) + (three[2 * chan : 3 * chan] + mb[layer])
            if final:
                base_last[b] = rest
            else:
                base[t, b] = rest
            return carry

        lax.fori_loop(0, blocks, per_block, 0, unroll=UNROLL)

    def moves(layer, hop, t):
        u = unit(layer, hop, t)
        return [
            pltpu.make_async_remote_copy(
                src_ref=sendb.at[u, o],
                dst_ref=pool_of(u).at[pl.ds(blocks + CAP * mirror[o], CAP)],
                send_sem=usend.at[u, o],
                recv_sem=urecv.at[u, mirror[o]],
                device_id={"sensor": peer},
                device_id_type=MESH,
            )
            for o, peer in enumerate(peers)
        ]

    def arrive(layer, hop, t):
        u = unit(layer, hop, t)
        for o, peer in enumerate(peers):
            copy = pltpu.make_async_remote_copy(
                src_ref=sendb.at[u, o],
                dst_ref=pool_of(u).at[pl.ds(blocks + CAP * o, CAP)],
                send_sem=usend.at[u, o],
                recv_sem=urecv.at[u, o],
                device_id={"sensor": peer},
                device_id_type=MESH,
            )
            copy.wait_recv()

    def send(layer, hop, t):
        u = unit(layer, hop, t)
        copies = moves(layer, hop, t)
        for o in range(len(peers)):
            for s in range(CAP):
                sendb[u, o, s] = fields[t, want[o][s]]
            copies[o].start()

    def diffuse(layer, hop, t):
        u = unit(layer, hop, t)

        def per_block(b, carry):
            picked = [pool_of(u)[src[k, b]] for k in range(maxt)]
            stack = jnp.concatenate(picked, axis=1)
            held = tiles_v[b].reshape(maxt * width, width)
            total = jnp.dot(stack, held, preferred_element_type=F32)
            if hop == 0:
                a = (mid[t, b] + total).astype(BF16)
                fields[t, b] = a
                pool_of(unit(layer, 1, t))[b] = a
            else:
                nxt = (base[t, b] + total).astype(BF16)
                into = x1 if layer == 0 else outv
                into[t, :, columns(b)] = nxt
            return carry

        lax.fori_loop(0, blocks, per_block, 0, unroll=UNROLL)

    def skip(t):
        def per_block(b, carry):
            out = jnp.dot(ws[...], hs[t, b], preferred_element_type=F32) + sb[...]
            skipv[t, :, columns(b)] = out.astype(BF16)
            return carry

        lax.fori_loop(0, blocks, per_block, 0, unroll=UNROLL)

    gate(0, early[0])

    first = unit(0, 0, early[0])

    def greet(final):
        for o, peer in enumerate(peers):

            @pl.when((peer > me) & ((peer == shards - 1) == final))
            def _():
                pl.semaphore_wait(here_sem.at[o], 1)
                tables[o].start()

    def wanted(o):
        asked = tab_r[o]
        row = CAP * mirror[o]
        return asked[row, 0], asked[row + 1, 0]

    def tell():
        @pl.when(root & below)
        def _():
            @pl.when(odd)
            def _():
                pl.semaphore_wait(known_sem, 1)

            for i in range(shards - 1):
                pl.semaphore_signal(
                    relay_sem.at[i], inc=1, device_id={"tm": before}, device_id_type=MESH
                )

    def pass_on():
        @pl.when(root & above)
        def _():
            for i in range(shards - 1):
                pl.semaphore_wait(relay_sem.at[i], 1)
                pl.semaphore_signal(
                    ready_sem, inc=1, device_id={"sensor": i + 1}, device_id_type=MESH
                )

    def serve(final):
        copies = moves(0, 0, early[0])
        for o, peer in enumerate(peers):

            @pl.when((peer == shards - 1) == final)
            def _():
                pltpu.make_async_remote_copy(
                    src_ref=req_v,
                    dst_ref=tab_r.at[o],
                    send_sem=tab_send.at[o],
                    recv_sem=tab_recv.at[o],
                    device_id={"sensor": peer},
                    device_id_type=MESH,
                ).wait_recv()

                for s, block in enumerate(wanted(o)):
                    sendb[first, o, s] = fields[early[0], block]
                copies[o].start()

    greet(False)
    greet(True)
    serve(False)
    serve(True)
    want = [wanted(o) for o in range(len(peers))]
    first_edge = pltpu.make_async_remote_copy(
        src_ref=series.at[steps - 1],
        dst_ref=edge0,
        send_sem=edge_send.at[0],
        recv_sem=edge_recv.at[0],
        device_id={"tm": after},
        device_id_type=MESH,
    )
    tiles_in.start()
    for t in range(steps):
        if t not in soon:
            parts[t].wait()
    for copy in loads[6:]:
        copy.wait()
    later_edges = [
        pltpu.make_async_remote_copy(
            src_ref=x1.at[steps - 2 + i],
            dst_ref=edge1.at[i],
            send_sem=edge_send.at[1 + i],
            recv_sem=edge_recv.at[1 + i],
            device_id={"tm": after},
            device_id_type=MESH,
        )
        for i in range(2)
    ]

    table = tab_v[...]
    rel, mine = bounds(table, me * blocks)
    place = jnp.where(mine, rel, dead)
    for o, peer in enumerate(peers):
        rel, mine = bounds(table, peer * blocks)
        place = jnp.where(mine, blocks + CAP * o + jnp.where(rel == leasts[o], 0, 1), place)
    place_v[...] = place
    places = pltpu.make_async_copy(place_v, src, place_sem)
    places.start()

    for t in early[1:]:
        if t == 0:

            if via:
                tell()

            @pl.when(jnp.logical_not(root & even) & above)
            def _():
                pl.semaphore_wait(ready_sem, 1)

            if via:
                pass_on()

            pl.when(above)(first_edge.start)
            pl.when(below)(first_edge.wait_recv)
        gate(0, t)
        send(0, 0, t)

    for u in range(last + 1):
        pool_of(u)[dead] = jnp.zeros((chan, width), BF16)
    for layer in range(1, LAYERS):
        prepare(layer)
    ws[...] = flipped([sw[layer] for layer in range(LAYERS)])
    row = sb_row[0:1, :]
    for layer in range(1, LAYERS):
        row = row + sb_row[pl.ds(layer, 1), :]
    for at in range(0, row.shape[1], 128):
        sb[at : at + 128] = upright(row[:, at : at + 128])

    places.wait()
    tiles_in.wait()
    done, sent = [], 0
    for t in early:
        arrive(0, 0, t)
        diffuse(0, 0, t)
        done.append(t)
        while sent < steps and order[sent] in done:
            send(0, 1, order[sent])
            sent += 1
    for t in order:
        arrive(0, 1, t)
        diffuse(0, 1, t)
        if t >= steps - 2:
            pl.when(above)(later_edges[t - (steps - 2)].start)
        else:
            gate(1, t + 2)
            send(1, 0, t + 2)
        if t < 2:
            pl.when(below)(later_edges[t].wait_recv)
            gate(1, t)
            send(1, 0, t)
    for t in order:
        skip(t)
    for t in order:
        arrive(1, 0, t)
        diffuse(1, 0, t)
        send(1, 1, t)
    for t in order[:-1]:
        arrive(1, 1, t)
        diffuse(1, 1, t)

    for copy in tables:
        copy.wait_send()

    @pl.when(above)
    def _():
        first_edge.wait_send()
        for copy in later_edges:
            copy.wait_send()

    for layer in range(LAYERS):
        for hop in range(HOPS):
            for t in order:
                u = unit(layer, hop, t)
                if u != last:
                    for copy in moves(layer, hop, t):
                        copy.wait_send()
    arrive(1, 1, order[-1])
    for copy in moves(1, 1, order[-1]):
        copy.wait_send()


def finish(
    outv, skipv, tiles_v, place_v, base, pool, stream, skip_sum, src, tail, sems
):
    steps, chan, nodes = outv.shape
    blocks, maxt, width = tiles_v.shape[0], tiles_v.shape[1], tiles_v.shape[2]
    order = order_of(steps)
    places = pltpu.make_async_copy(place_v, src, sems.at[0])
    places.start()
    copies = [pltpu.make_async_copy(skipv, skip_sum, sems.at[1])]
    for i, t in enumerate(order[:-1]):
        copies.append(pltpu.make_async_copy(outv.at[t], stream.at[t], sems.at[2 + i]))
    for copy in copies:
        copy.start()
    places.wait()

    def per_block(b, carry):
        stack = jnp.concatenate([pool[src[k, b]] for k in range(maxt)], axis=1)
        held = tiles_v[b].reshape(maxt * width, width)
        total = jnp.dot(stack, held, preferred_element_type=F32)
        cols = pl.ds(pl.multiple_of(b * width, width), width)
        tail[:, cols] = (base[b] + total).astype(BF16)
        return carry

    lax.fori_loop(0, blocks, per_block, 0, unroll=UNROLL)
    final = pltpu.make_async_copy(tail, stream.at[order[-1]], sems.at[1 + steps])
    final.start()
    for copy in copies:
        copy.wait()
    final.wait()


def solution(mesh):
    shards, ranks = mesh.shape["sensor"], mesh.shape["tm"]
    links = len(offsets_of(shards))

    def on_device(
        series, neighbours, tile_count, tiles, fgw, fgb, skip_weight, skip_b, hop_mixing, mix_b
    ):
        steps, chan, nodes = series.shape
        blocks, maxt, width = tiles.shape[0], tiles.shape[1], tiles.shape[2]
        wide = skip_weight.shape[1]
        pool = blocks + CAP * links + 1
        units = LAYERS * HOPS * steps
        fgw_t = jnp.swapaxes(fgw, 2, 3)
        skip_t = jnp.swapaxes(skip_weight, 1, 2)
        operands = [
            pltpu.with_memory_space_constraint(held, pltpu.HBM)
            for held in (
                neighbours.T,
                tile_count[None, :],
                series,
                tiles,
                fgw_t,
                fgb,
                skip_t,
                skip_b,
                hop_mixing,
                mix_b,
            )
        ]
        vmem = pl.BlockSpec(memory_space=pltpu.VMEM)
        hbm = pl.BlockSpec(memory_space=pltpu.HBM)
        dma = pltpu.SemaphoreType.DMA
        results = (
            jax.ShapeDtypeStruct(series.shape, BF16),
            jax.ShapeDtypeStruct((steps, wide, nodes), BF16),
        )
        held = pl.pallas_call(
            functools.partial(body, shards, ranks),
            out_shape=results
            + (
                jax.ShapeDtypeStruct(tiles.shape, BF16),
                jax.ShapeDtypeStruct((8, 128), jnp.int32),
                jax.ShapeDtypeStruct((blocks, chan, width), F32),
                jax.ShapeDtypeStruct((pool, chan, width), BF16),
            ),
            in_specs=[hbm] * 10,
            out_specs=(vmem,) * 6,
            scratch_shapes=[
                pltpu.VMEM((maxt, blocks), jnp.int32),
                pltpu.VMEM((1, blocks), jnp.int32),
                pltpu.VMEM((8, 128), jnp.int32),
                pltpu.VMEM((8, 128), jnp.int32),
                pltpu.VMEM((links, 8, 128), jnp.int32),
                pltpu.SMEM((8, 128), jnp.int32),
                pltpu.VMEM(series.shape, BF16),
                pltpu.VMEM(fgw_t.shape, BF16),
                pltpu.VMEM(fgb.shape, F32),
                pltpu.VMEM(skip_t.shape, BF16),
                pltpu.VMEM(skip_b.shape, F32),
                pltpu.VMEM(hop_mixing.shape, BF16),
                pltpu.VMEM(mix_b.shape, F32),
                pltpu.VMEM((LAYERS, 2 * chan, width), F32),
                pltpu.VMEM((wide, width), F32),
                pltpu.VMEM((LAYERS, chan, width), F32),
                pltpu.VMEM(series.shape, BF16),
                pltpu.VMEM((chan, nodes), BF16),
                pltpu.VMEM((2, chan, nodes), BF16),
                pltpu.VMEM((steps, blocks, chan, width), BF16),
                pltpu.VMEM((steps, blocks, chan, width), F32),
                pltpu.VMEM((steps, blocks, chan, width), F32),
                pltpu.VMEM((steps, blocks, LAYERS * chan, width), BF16),
                pltpu.VMEM((units, links, CAP, chan, width), BF16),
                pltpu.VMEM((LAYERS, 2 * chan, 2 * chan), BF16),
                pltpu.VMEM((LAYERS, 3 * chan, chan), BF16),
                pltpu.VMEM((wide, LAYERS * chan), BF16),
                dma,
                dma((8,)),
                dma((steps,)),
                dma((links,)),
                dma((links,)),
                dma,
                pltpu.SemaphoreType.REGULAR,
                pltpu.SemaphoreType.REGULAR,
                pltpu.SemaphoreType.REGULAR((3,)),
                pltpu.SemaphoreType.REGULAR((links,)),
                dma((3,)),
                dma((3,)),
                dma((units, links)),
                dma((units, links)),
            ]
            + [pltpu.VMEM((pool, chan, width), BF16)] * (units - 1),
            compiler_params=pltpu.CompilerParams(
                collective_id=0, has_side_effects=True, vmem_limit_bytes=40 << 20
            ),
        )(*operands)
        return pl.pallas_call(
            finish,
            out_shape=results,
            in_specs=[vmem] * 6,
            out_specs=(hbm, hbm),
            scratch_shapes=[
                pltpu.SMEM((8, 128), jnp.int32),
                pltpu.VMEM((chan, nodes), BF16),
                dma((2 + steps,)),
            ],
            compiler_params=pltpu.CompilerParams(vmem_limit_bytes=4 << 20),
        )(*held)

    return jax.shard_map(
        on_device,
        mesh=mesh,
        in_specs=(
            P("tm", None, ("groups", "sensor")),
            P(("groups", "sensor"), None),
            P(("groups", "sensor")),
            P(("groups", "sensor"), None, None, None),
            P(),
            P(),
            P(),
            P(),
            P(),
            P(),
        ),
        out_specs=(P("tm", None, ("groups", "sensor")), P("tm", None, ("groups", "sensor"))),
        check_vma=False,
    )
```

```python
import functools

import jax
import jax.numpy as jnp
from jax import lax
from jax.experimental import pallas as pl
from jax.experimental.pallas import tpu as pltpu
from jax.sharding import PartitionSpec as P

CAP = 2
LAYERS = 2
HOPS = 2
UNROLL = 8
MESH = pl.DeviceIdType.MESH
F32 = jnp.float32
BF16 = jnp.bfloat16


def offsets_of(shards):
    found = []
    for step in (2, shards - 2, 1, shards - 1):
        step = step % shards
        if step and step not in found:
            found.append(step)
    return found


def order_of(steps):
    return list(range(steps - 1, -1, -2)) + list(range(steps - 2, -1, -2))


def body(
    shards,
    ranks,
    near_hbm,
    count_hbm,
    series_hbm,
    tiles_hbm,
    fgw_hbm,
    fgb_hbm,
    sw_hbm,
    sb_hbm,
    hmw_hbm,
    mb_hbm,
    outv,
    skipv,
    tiles_v,
    place_v,
    base_last,
    pool_last,
    w_last,
    near,
    count,
    tab_v,
    req_v,
    tab_r,
    src,
    series,
    fgw,
    fgb_row,
    sw,
    sb_row,
    hmw,
    mb_row,
    fgb,
    sb,
    mb,
    x1,
    edge0,
    edge1,
    fields,
    base,
    hs,
    sendb,
    wg,
    wm,
    ws,
    tiles_sem,
    load_sem,
    series_sem,
    tab_send,
    tab_recv,
    place_sem,
    ready_sem,
    here_sem,
    edge_send,
    edge_recv,
    usend,
    urecv,
    *pools,
):
    steps, chan, nodes = series.shape
    blocks, maxt, width = tiles_v.shape[0], tiles_v.shape[1], tiles_v.shape[2]
    offs = offsets_of(shards)
    order = order_of(steps)
    early = list(range(steps - 1, -1, -1))
    me = lax.axis_index("sensor")
    tm = lax.axis_index("tm")
    peers = [lax.rem(me + off, shards) for off in offs]
    mirror = [offs.index(shards - off) for off in offs]
    after = lax.rem(tm + 1, ranks)
    before = lax.rem(tm + ranks - 1, ranks)
    even = lax.rem(tm, 2) == 0
    odd = jnp.logical_not(even)
    above, below = tm < ranks - 1, tm > 0
    dead = blocks + CAP * len(offs)
    last = LAYERS * HOPS * steps - 1

    def unit(layer, hop, t):
        return (layer * HOPS + hop) * steps + order.index(t)

    def pool_of(u):
        return pool_last if u == last else pools[u]

    def bounds(table, low):
        rel = table - low
        mine = (rel >= 0) & (rel < blocks)
        return rel, mine

    barrier = pltpu.get_barrier_semaphore()
    for peer in peers:

        @pl.when(peer > me)
        def _():
            pl.semaphore_signal(barrier, inc=1, device_id={"sensor": peer}, device_id_type=MESH)


    @pl.when(odd & above)
    def _():
        pl.semaphore_signal(barrier, inc=1, device_id={"tm": after}, device_id_type=MESH)

    @pl.when(odd & below)
    def _():
        pl.semaphore_signal(barrier, inc=1, device_id={"tm": before}, device_id_type=MESH)

    loads = [
        pltpu.make_async_copy(held, into, load_sem.at[i])
        for i, (held, into) in enumerate(
            (
                (near_hbm, near),
                (count_hbm, count),
                (fgw_hbm, fgw),
                (fgb_hbm, fgb_row),
                (hmw_hbm, hmw),
                (mb_hbm, mb_row),
                (sw_hbm, sw),
                (sb_hbm, sb_row),
            )
        )
    ]
    parts = [
        pltpu.make_async_copy(series_hbm.at[t], series.at[t], series_sem.at[t])
        for t in range(steps)
    ]
    soon = [early[0], early[0] - 1]
    for copy in loads[:2]:
        copy.start()
    for t in soon:
        parts[t].start()
    for copy in loads[2:6]:
        copy.start()
    for t in range(steps - 1, -1, -1):
        if t not in soon:
            parts[t].start()
    for copy in loads[6:]:
        copy.start()
    tiles_in = pltpu.make_async_copy(tiles_hbm, tiles_v, tiles_sem)

    lower = sum([jnp.where(peer < me, 1, 0) for peer in peers])
    beside = jnp.where(above, 1, 0) + jnp.where(below, 1, 0)
    greeted = lower + jnp.where(even, beside, 0)

    @pl.when(greeted > 0)
    def _():
        pl.semaphore_wait(barrier, greeted)

    for o, peer in enumerate(peers):

        @pl.when(peer < me)
        def _():
            pl.semaphore_signal(
                here_sem.at[mirror[o]], inc=1, device_id={"sensor": peer}, device_id_type=MESH
            )

    @pl.when(even & below)
    def _():
        pl.semaphore_signal(ready_sem, inc=1, device_id={"tm": before}, device_id_type=MESH)

    loads[0].wait()
    loads[1].wait()
    slot = lax.broadcasted_iota(jnp.int32, near.shape, 0)
    tab_v[...] = jnp.full(tab_v.shape, -1, jnp.int32)
    table = jnp.where(slot < count[...], near[...], -1)
    tab_v[0:maxt, 0:blocks] = table
    line = lax.broadcasted_iota(jnp.int32, req_v.shape, 0)
    leasts, asks = [], jnp.zeros(req_v.shape, jnp.int32)
    for o, peer in enumerate(peers):
        rel, mine = bounds(table, peer * blocks)
        least = jnp.min(jnp.where(mine, rel, blocks), axis=(0, 1), keepdims=True)
        most = jnp.max(jnp.where(mine, rel, -1), axis=(0, 1), keepdims=True)
        leasts.append(least)
        asks = jnp.where(line == CAP * o, jnp.where(least < blocks, least, 0), asks)
        asks = jnp.where(line == CAP * o + 1, jnp.maximum(most, 0), asks)
    req_v[...] = asks

    tables = [
        pltpu.make_async_remote_copy(
            src_ref=req_v,
            dst_ref=tab_r.at[mirror[o]],
            send_sem=tab_send.at[o],
            recv_sem=tab_recv.at[mirror[o]],
            device_id={"sensor": peer},
            device_id_type=MESH,
        )
        for o, peer in enumerate(peers)
    ]
    for o, peer in enumerate(peers):
        pl.when(peer < me)(tables[o].start)

    for copy in loads[2:6]:
        copy.wait()

    def upright(row):
        tall = jnp.transpose(jnp.broadcast_to(row, (128, 128)))
        return jnp.concatenate([tall] * (width // 128), axis=1)

    def flipped(parts):
        return jnp.transpose(jnp.concatenate(parts, axis=0).astype(F32)).astype(BF16)

    both_mix = upright(jnp.concatenate([mb_row[pl.ds(i, 1), :] for i in range(LAYERS)], axis=1))
    for layer in range(LAYERS):
        mb[layer] = both_mix[layer * chan : (layer + 1) * chan]

    def prepare(layer):
        fgb[layer] = upright(fgb_row[pl.ds(layer, 1), :])
        wg[layer] = flipped([fgw[layer, 0], fgw[layer, 1]])
        w = hmw[layer]
        for i in range(3):
            wm[layer, i] = w[:, i * chan : (i + 1) * chan]
        if layer == LAYERS - 1:
            w_last[...] = wm[layer, 2]

    prepare(0)
    for t in soon:
        parts[t].wait()

    def columns(b):
        return pl.ds(pl.multiple_of(b * width, width), width)

    def gate(layer, t):
        reach = 2**layer
        field = series if layer == 0 else x1
        u = unit(layer, 0, t)

        def per_block(b, carry):
            cols = columns(b)
            cur = field[t, :, cols]
            if t >= reach:
                prev = field[t - reach, :, cols]
            else:
                held = edge0[:, cols] if layer == 0 else edge1[t, :, cols]
                prev = lax.select(below, held, jnp.zeros_like(held))
            both = jnp.concatenate([prev, cur], axis=0)
            pre = jnp.dot(wg[layer], both, preferred_element_type=F32) + fgb[layer]
            half = pre.shape[0] // 2
            h = jnp.tanh(pre[:half]) * (0.5 * jnp.tanh(0.5 * pre[half:]) + 0.5)
            h = h.astype(BF16)
            hs[t, b, layer * chan : (layer + 1) * chan] = h
            fields[t, b] = h
            pool_of(u)[b] = h
            part = jnp.dot(wm[layer, 0], h, preferred_element_type=F32)
            base[t, b] = cur.astype(F32) + (part + mb[layer])
            return carry

        lax.fori_loop(0, blocks, per_block, 0, unroll=UNROLL)

    def moves(layer, hop, t):
        u = unit(layer, hop, t)
        return [
            pltpu.make_async_remote_copy(
                src_ref=sendb.at[u, o],
                dst_ref=pool_of(u).at[pl.ds(blocks + CAP * mirror[o], CAP)],
                send_sem=usend.at[u, o],
                recv_sem=urecv.at[u, mirror[o]],
                device_id={"sensor": peer},
                device_id_type=MESH,
            )
            for o, peer in enumerate(peers)
        ]

    def arrive(layer, hop, t):
        u = unit(layer, hop, t)
        for o, peer in enumerate(peers):
            copy = pltpu.make_async_remote_copy(
                src_ref=sendb.at[u, o],
                dst_ref=pool_of(u).at[pl.ds(blocks + CAP * o, CAP)],
                send_sem=usend.at[u, o],
                recv_sem=urecv.at[u, o],
                device_id={"sensor": peer},
                device_id_type=MESH,
            )
            copy.wait_recv()

    def send(layer, hop, t):
        u = unit(layer, hop, t)
        copies = moves(layer, hop, t)
        for o in range(len(peers)):
            for s in range(CAP):
                sendb[u, o, s] = fields[t, want[o][s]]
            copies[o].start()

    def diffuse(layer, hop, t):
        u = unit(layer, hop, t)

        def per_block(b, carry):
            picked = [pool_of(u)[src[k, b]] for k in range(maxt)]
            stack = jnp.concatenate(picked, axis=1)
            held = tiles_v[b].reshape(maxt * width, width)
            total = jnp.dot(stack, held, preferred_element_type=F32)
            a = total.astype(BF16)
            fields[t, b] = a
            if hop == 0:
                pool_of(unit(layer, 1, t))[b] = a
            return carry

        lax.fori_loop(0, blocks, per_block, 0, unroll=UNROLL)

    def blend(layer, hop, t):
        final = unit(layer, 1, t) == last

        def per_block(b, carry):
            part = jnp.dot(wm[layer, hop + 1], fields[t, b], preferred_element_type=F32)
            rest = base[t, b] + part
            if hop == 1:
                into = x1 if layer == 0 else outv
                into[t, :, columns(b)] = rest.astype(BF16)
            elif final:
                base_last[b] = rest
            else:
                base[t, b] = rest
            return carry

        lax.fori_loop(0, blocks, per_block, 0, unroll=UNROLL)

    def skip(t):
        def per_block(b, carry):
            out = jnp.dot(ws[...], hs[t, b], preferred_element_type=F32) + sb[...]
            skipv[t, :, columns(b)] = out.astype(BF16)
            return carry

        lax.fori_loop(0, blocks, per_block, 0, unroll=UNROLL)

    gate(0, early[0])

    first = unit(0, 0, early[0])

    def greet(final):
        for o, peer in enumerate(peers):

            @pl.when((peer > me) & ((peer == shards - 1) == final))
            def _():
                pl.semaphore_wait(here_sem.at[o], 1)
                tables[o].start()

    def wanted(o):
        asked = tab_r[o]
        row = CAP * mirror[o]
        return asked[row, 0], asked[row + 1, 0]

    def serve(final):
        copies = moves(0, 0, early[0])
        for o, peer in enumerate(peers):

            @pl.when((peer == shards - 1) == final)
            def _():
                pltpu.make_async_remote_copy(
                    src_ref=req_v,
                    dst_ref=tab_r.at[o],
                    send_sem=tab_send.at[o],
                    recv_sem=tab_recv.at[o],
                    device_id={"sensor": peer},
                    device_id_type=MESH,
                ).wait_recv()

                for s, block in enumerate(wanted(o)):
                    sendb[first, o, s] = fields[early[0], block]
                copies[o].start()

    greet(False)
    greet(True)
    serve(False)
    serve(True)
    want = [wanted(o) for o in range(len(peers))]
    first_edge = pltpu.make_async_remote_copy(
        src_ref=series.at[steps - 1],
        dst_ref=edge0,
        send_sem=edge_send.at[0],
        recv_sem=edge_recv.at[0],
        device_id={"tm": after},
        device_id_type=MESH,
    )
    tiles_in.start()
    for t in range(steps):
        if t not in soon:
            parts[t].wait()
    for copy in loads[6:]:
        copy.wait()
    later_edges = [
        pltpu.make_async_remote_copy(
            src_ref=x1.at[steps - 2 + i],
            dst_ref=edge1.at[i],
            send_sem=edge_send.at[1 + i],
            recv_sem=edge_recv.at[1 + i],
            device_id={"tm": after},
            device_id_type=MESH,
        )
        for i in range(2)
    ]

    table = tab_v[...]
    rel, mine = bounds(table, me * blocks)
    place = jnp.where(mine, rel, dead)
    for o, peer in enumerate(peers):
        rel, mine = bounds(table, peer * blocks)
        place = jnp.where(mine, blocks + CAP * o + jnp.where(rel == leasts[o], 0, 1), place)
    place_v[...] = place
    places = pltpu.make_async_copy(place_v, src, place_sem)
    places.start()

    for t in early[1:]:
        if t == 0:

            @pl.when(odd & above)
            def _():
                pl.semaphore_wait(ready_sem, 1)

            pl.when(above)(first_edge.start)
            pl.when(below)(first_edge.wait_recv)
        gate(0, t)
        send(0, 0, t)

    for u in range(last + 1):
        pool_of(u)[dead] = jnp.zeros((chan, width), BF16)
    for layer in range(1, LAYERS):
        prepare(layer)
    ws[...] = flipped([sw[layer] for layer in range(LAYERS)])
    row = sb_row[0:1, :]
    for layer in range(1, LAYERS):
        row = row + sb_row[pl.ds(layer, 1), :]
    for at in range(0, row.shape[1], 128):
        sb[at : at + 128] = upright(row[:, at : at + 128])

    places.wait()
    tiles_in.wait()
    done, sent = [], 0
    for t in early:
        arrive(0, 0, t)
        diffuse(0, 0, t)
        done.append(t)
        while sent < steps and order[sent] in done:
            send(0, 1, order[sent])
            blend(0, 0, order[sent])
            sent += 1
    for t in order:
        arrive(0, 1, t)
        diffuse(0, 1, t)
        blend(0, 1, t)
        if t >= steps - 2:
            pl.when(above)(later_edges[t - (steps - 2)].start)
        else:
            gate(1, t + 2)
            send(1, 0, t + 2)
        if t < 2:
            pl.when(below)(later_edges[t].wait_recv)
            gate(1, t)
            send(1, 0, t)
    for t in order:
        skip(t)
    for t in order:
        arrive(1, 0, t)
        diffuse(1, 0, t)
        send(1, 1, t)
        blend(1, 0, t)
    for t in order[:-1]:
        arrive(1, 1, t)
        diffuse(1, 1, t)
        blend(1, 1, t)

    for copy in tables:
        copy.wait_send()

    @pl.when(above)
    def _():
        first_edge.wait_send()
        for copy in later_edges:
            copy.wait_send()

    for layer in range(LAYERS):
        for hop in range(HOPS):
            for t in order:
                u = unit(layer, hop, t)
                if u != last:
                    for copy in moves(layer, hop, t):
                        copy.wait_send()
    arrive(1, 1, order[-1])
    for copy in moves(1, 1, order[-1]):
        copy.wait_send()


def finish(
    outv, skipv, tiles_v, place_v, base, pool, w, stream, skip_sum, src, hold, tail, sems
):
    steps, chan, nodes = outv.shape
    blocks, maxt, width = tiles_v.shape[0], tiles_v.shape[1], tiles_v.shape[2]
    order = order_of(steps)
    places = pltpu.make_async_copy(place_v, src, sems.at[0])
    places.start()
    copies = [pltpu.make_async_copy(skipv, skip_sum, sems.at[1])]
    for i, t in enumerate(order[:-1]):
        copies.append(pltpu.make_async_copy(outv.at[t], stream.at[t], sems.at[2 + i]))
    for copy in copies:
        copy.start()
    places.wait()

    def per_block(b, carry):
        stack = jnp.concatenate([pool[src[k, b]] for k in range(maxt)], axis=1)
        held = tiles_v[b].reshape(maxt * width, width)
        total = jnp.dot(stack, held, preferred_element_type=F32)
        hold[b] = total.astype(BF16)
        return carry

    def blend(b, carry):
        cols = pl.ds(pl.multiple_of(b * width, width), width)
        part = jnp.dot(w[...], hold[b], preferred_element_type=F32)
        tail[:, cols] = (base[b] + part).astype(BF16)
        return carry

    lax.fori_loop(0, blocks, per_block, 0, unroll=UNROLL)
    lax.fori_loop(0, blocks, blend, 0, unroll=UNROLL)
    final = pltpu.make_async_copy(tail, stream.at[order[-1]], sems.at[1 + steps])
    final.start()
    for copy in copies:
        copy.wait()
    final.wait()


def solution(mesh):
    shards, ranks = mesh.shape["sensor"], mesh.shape["tm"]
    links = len(offsets_of(shards))

    def on_device(
        series, neighbours, tile_count, tiles, fgw, fgb, skip_weight, skip_b, hop_mixing, mix_b
    ):
        steps, chan, nodes = series.shape
        blocks, maxt, width = tiles.shape[0], tiles.shape[1], tiles.shape[2]
        wide = skip_weight.shape[1]
        pool = blocks + CAP * links + 1
        units = LAYERS * HOPS * steps
        fgw_t = jnp.swapaxes(fgw, 2, 3)
        skip_t = jnp.swapaxes(skip_weight, 1, 2)
        operands = [
            pltpu.with_memory_space_constraint(held, pltpu.HBM)
            for held in (
                neighbours.T,
                tile_count[None, :],
                series,
                tiles,
                fgw_t,
                fgb,
                skip_t,
                skip_b,
                hop_mixing,
                mix_b,
            )
        ]
        vmem = pl.BlockSpec(memory_space=pltpu.VMEM)
        hbm = pl.BlockSpec(memory_space=pltpu.HBM)
        dma = pltpu.SemaphoreType.DMA
        results = (
            jax.ShapeDtypeStruct(series.shape, BF16),
            jax.ShapeDtypeStruct((steps, wide, nodes), BF16),
        )
        held = pl.pallas_call(
            functools.partial(body, shards, ranks),
            out_shape=results
            + (
                jax.ShapeDtypeStruct(tiles.shape, BF16),
                jax.ShapeDtypeStruct((8, 128), jnp.int32),
                jax.ShapeDtypeStruct((blocks, chan, width), F32),
                jax.ShapeDtypeStruct((pool, chan, width), BF16),
                jax.ShapeDtypeStruct((chan, chan), BF16),
            ),
            in_specs=[hbm] * 10,
            out_specs=(vmem,) * 7,
            scratch_shapes=[
                pltpu.VMEM((maxt, blocks), jnp.int32),
                pltpu.VMEM((1, blocks), jnp.int32),
                pltpu.VMEM((8, 128), jnp.int32),
                pltpu.VMEM((8, 128), jnp.int32),
                pltpu.VMEM((links, 8, 128), jnp.int32),
                pltpu.SMEM((8, 128), jnp.int32),
                pltpu.VMEM(series.shape, BF16),
                pltpu.VMEM(fgw_t.shape, BF16),
                pltpu.VMEM(fgb.shape, F32),
                pltpu.VMEM(skip_t.shape, BF16),
                pltpu.VMEM(skip_b.shape, F32),
                pltpu.VMEM(hop_mixing.shape, BF16),
                pltpu.VMEM(mix_b.shape, F32),
                pltpu.VMEM((LAYERS, 2 * chan, width), F32),
                pltpu.VMEM((wide, width), F32),
                pltpu.VMEM((LAYERS, chan, width), F32),
                pltpu.VMEM(series.shape, BF16),
                pltpu.VMEM((chan, nodes), BF16),
                pltpu.VMEM((2, chan, nodes), BF16),
                pltpu.VMEM((steps, blocks, chan, width), BF16),
                pltpu.VMEM((steps, blocks, chan, width), F32),
                pltpu.VMEM((steps, blocks, LAYERS * chan, width), BF16),
                pltpu.VMEM((units, links, CAP, chan, width), BF16),
                pltpu.VMEM((LAYERS, 2 * chan, 2 * chan), BF16),
                pltpu.VMEM((LAYERS, 3, chan, chan), BF16),
                pltpu.VMEM((wide, LAYERS * chan), BF16),
                dma,
                dma((8,)),
                dma((steps,)),
                dma((links,)),
                dma((links,)),
                dma,
                pltpu.SemaphoreType.REGULAR,
                pltpu.SemaphoreType.REGULAR((links,)),
                dma((3,)),
                dma((3,)),
                dma((units, links)),
                dma((units, links)),
            ]
            + [pltpu.VMEM((pool, chan, width), BF16)] * (units - 1),
            compiler_params=pltpu.CompilerParams(
                collective_id=0, has_side_effects=True, vmem_limit_bytes=40 << 20
            ),
        )(*operands)
        return pl.pallas_call(
            finish,
            out_shape=results,
            in_specs=[vmem] * 7,
            out_specs=(hbm, hbm),
            scratch_shapes=[
                pltpu.SMEM((8, 128), jnp.int32),
                pltpu.VMEM((blocks, chan, width), BF16),
                pltpu.VMEM((chan, nodes), BF16),
                dma((2 + steps,)),
            ],
            compiler_params=pltpu.CompilerParams(vmem_limit_bytes=4 << 20),
        )(*held)

    return jax.shard_map(
        on_device,
        mesh=mesh,
        in_specs=(
            P("tm", None, ("groups", "sensor")),
            P(("groups", "sensor"), None),
            P(("groups", "sensor")),
            P(("groups", "sensor"), None, None, None),
            P(),
            P(),
            P(),
            P(),
            P(),
            P(),
        ),
        out_specs=(P("tm", None, ("groups", "sensor")), P("tm", None, ("groups", "sensor"))),
        check_vma=False,
    )
```
